256 devices in a mesh: batch: 64 (over z_hi, x, y), seq: 4 (over z_lo, core).
Axes of the slice: x: 4, y: 4, z: 8 (z_hi: 4, z_lo: 2; z = z_hi * 2 + z_lo), core: 2. Of those that a mesh axis runs over, the one named last changes fastest.
Arguments:
- embedded: bfloat16 [64, 2048, 768], P('batch', 'seq'), may hold values from -6 to 6
- conv_weight: bfloat16 [2304, 768], replicated, may hold values from -0.125 to 0.125
- qkv_weight: bfloat16 [1536, 1792], replicated, may hold values from -0.15625 to 0.15625
- cotangent: bfloat16 [64, 1024, 768], P('batch', 'seq'), may hold values from -6 to 6
Outputs:
- attended: bfloat16 [64, 1024, 768], P('batch', 'seq')
- grad_conv: float32 [2304, 768], P('batch')
- grad_qkv: float32 [1536, 1792], P('batch')
The draws below stay inside these ranges and needn't reach their ends.
All inputs are finite; a program needn't handle non-finite values.
Results may differ from the reference program's by a relative error of at most 0.012.
Values may be sent and summed in bfloat16 or wider, within the bound.
No kernel may reach another device: no remote copies, remote signals or barrier semaphores. Data moves between devices by JAX's collectives and lax.ppermute only.
A program may use at most 128 MiB of HBM per device.

```python
import math
import jax
import jax.numpy as jnp
from jax import lax

C = 768
HEADS = 4
HK = 128
HV = 192
DILATION_STEP = 4
D = 1536
QKV = 1792
SEQ_LEN = 2048
ATT_LEN = 1024
N_BATCH = 64


def block_levels(rng, extent, shards, low, largest):
    level = 1.0
    for position, parts in shards:
        heights = jax.random.uniform(jax.random.fold_in(jax.random.fold_in(rng, 6), position), (parts,), jnp.float32, low / len(shards), largest / len(shards))
        level = level * jnp.repeat(jnp.exp(heights), extent[position] // parts).reshape((-1,) + (1,) * (len(extent) - 1 - position))
    return level


def noise(stream_key, dims, spread, bound, shards=(), dtype=jnp.bfloat16):
    array = jax.random.normal(stream_key, dims, jnp.float32) * spread
    if len(shards) > 0:
        array = block_levels(stream_key, dims, shards, -0.22, 0.18) * array
    return jnp.clip(array, min=-bound, max=bound).astype(dtype)


def setup_inputs(seed: int = 0) -> dict:
    key_of = jax.random.split(jax.random.key(seed), 5)
    embedded = noise(key_of[0], (N_BATCH, SEQ_LEN, C), 1.0, 6.0, ((0, 64), (1, 4)))
    conv_weight = noise(key_of[1], (3 * C, C), (3 * C) ** -0.5, 0.125)
    qkv_weight = noise(key_of[2], (D, QKV), D ** -0.5, 0.15625)
    cotangent = noise(key_of[3], (N_BATCH, ATT_LEN, HEADS * HV), 1.0, 6.0, ((0, 64), (1, 4)))
    return {"embedded": embedded, "conv_weight": conv_weight, "qkv_weight": qkv_weight, "cotangent": cotangent}


epsilon = 1e-06

def normalize(raw_rows):
    factor = lax.rsqrt(lax.optimization_barrier(jnp.mean(raw_rows * raw_rows, axis=-1, keepdims=True)) + epsilon)
    return ((raw_rows * factor).astype(jnp.bfloat16), factor)

def normalize_back(raw_rows, factor, grad_normed):
    grad_f = grad_normed.astype(jnp.float32)
    inner = lax.optimization_barrier(jnp.mean(grad_f * raw_rows, axis=-1, keepdims=True))
    return (factor * grad_f - raw_rows * factor * factor * factor * inner).astype(jnp.bfloat16)

def one_window(embedded, conv_weight, qkv_weight, grad_row):
    position_index = embedded.shape[0]
    channels = embedded.shape[1]
    half_rows = position_index // 2
    gelu_output = jax.nn.gelu(embedded.astype(jnp.float32), approximate=True).astype(jnp.bfloat16)
    padded_input = jnp.pad(gelu_output, ((DILATION_STEP, DILATION_STEP), (0, 0)))
    stacked_taps = jnp.concatenate([padded_input[kernel_tap * DILATION_STEP:kernel_tap * DILATION_STEP + position_index] for kernel_tap in range(3)], axis=1)
    conv_out = jnp.dot(stacked_taps, conv_weight, preferred_element_type=jnp.float32)
    hidden = (embedded.astype(jnp.float32) + conv_out).astype(jnp.bfloat16)
    joined = hidden.reshape(half_rows, 2 * channels)
    projected = jnp.dot(joined, qkv_weight, preferred_element_type=jnp.float32)
    query_raw = projected[:, :HEADS * HK].reshape(half_rows, HEADS, HK)
    key_raw = projected[:, HEADS * HK:2 * HEADS * HK].reshape(half_rows, HEADS, HK)
    value_rows = projected[:, 2 * HEADS * HK:].reshape(half_rows, HEADS, HV).astype(jnp.bfloat16)
    query_n, query_factor = normalize(query_raw)
    key_n, key_factor = normalize(key_raw)
    temper = 1.0 / math.sqrt(HK)
    scores = jnp.einsum('qhd,khd->hqk', query_n.astype(jnp.float32), key_n.astype(jnp.float32)) * temper
    expo = jnp.exp(scores)
    probs = expo / lax.optimization_barrier(jnp.sum(expo, axis=-1, keepdims=True))
    probs_b = probs.astype(jnp.bfloat16)
    attended = jnp.einsum('hqk,khd->qhd', probs_b.astype(jnp.float32), value_rows.astype(jnp.float32)).astype(jnp.bfloat16)
    grad_in = grad_row.reshape(half_rows, HEADS, HV)
    grad_value = jnp.einsum('hqk,qhd->khd', probs_b.astype(jnp.float32), grad_in.astype(jnp.float32)).astype(jnp.bfloat16)
    grad_probs = jnp.einsum('qhd,khd->hqk', grad_in.astype(jnp.float32), value_rows.astype(jnp.float32))
    inner = lax.optimization_barrier(jnp.sum(probs * grad_probs, axis=-1, keepdims=True))
    grad_scores = (probs * (grad_probs - inner) * temper).astype(jnp.bfloat16)
    grad_query_n = jnp.einsum('hqk,khd->qhd', grad_scores.astype(jnp.float32), key_n.astype(jnp.float32)).astype(jnp.bfloat16)
    grad_key_n = jnp.einsum('hqk,qhd->khd', grad_scores.astype(jnp.float32), query_n.astype(jnp.float32)).astype(jnp.bfloat16)
    grad_query = normalize_back(query_raw, query_factor, grad_query_n)
    grad_key = normalize_back(key_raw, key_factor, grad_key_n)
    grad_proj = jnp.concatenate([grad_query.reshape(half_rows, HEADS * HK), grad_key.reshape(half_rows, HEADS * HK), grad_value.reshape(half_rows, HEADS * HV)], axis=1)
    qkv_weight_sum = jnp.dot(joined.T, grad_proj, preferred_element_type=jnp.float32)
    grad_joined = jnp.dot(grad_proj, qkv_weight.T, preferred_element_type=jnp.float32).astype(jnp.bfloat16)
    grad_hidden = grad_joined.reshape(position_index, channels)
    conv_term = jnp.dot(stacked_taps.T, grad_hidden, preferred_element_type=jnp.float32)
    return (attended.reshape(half_rows, HEADS * HV), conv_term, qkv_weight_sum)

def reference(embedded, conv_weight, qkv_weight, cotangent):

    def step(carry, inputs):
        window_rows, grad_row = inputs
        attended, conv_term, qkv_weight_sum = one_window(window_rows, conv_weight, qkv_weight, grad_row)
        return ((carry[0] + conv_term, carry[1] + qkv_weight_sum), attended)
    start = (jnp.zeros(conv_weight.shape, jnp.float32), jnp.zeros(qkv_weight.shape, jnp.float32))
    totals, attended = lax.scan(step, start, (embedded, cotangent))
    return (attended, totals[0], totals[1])
```

```python
import math

import jax
import jax.numpy as jnp
from jax import lax
from jax.sharding import PartitionSpec as P

HEADS = 4
HK = 128
HV = 192
HD = 2 * HK + HV
STEP = 4
GRID = (4, 4, 4)
F32 = jnp.float32
BF16 = jnp.bfloat16

epsilon = 1e-06
temper = 1.0 / math.sqrt(HK)


def swap_seq(block, mask):
    return lax.ppermute(block, "seq", [(i, i ^ mask) for i in range(4)])


def shift_batch(block, axis, distance):
    pairs = []
    for b in range(64):
        place = [b // 16, (b // 4) % 4, b % 4]
        place[axis] = (place[axis] + distance) % 4
        pairs.append((b, place[0] * 16 + place[1] * 4 + place[2]))
    return lax.ppermute(block, "batch", pairs)


def pick(array, index, axis=0):
    return lax.dynamic_index_in_dim(array, index, axis, keepdims=False)


def normalize(raw_rows):
    factor = lax.rsqrt(jnp.mean(raw_rows * raw_rows, axis=-1, keepdims=True) + epsilon)
    return ((raw_rows * factor).astype(BF16), factor)


def normalize_back(raw_rows, factor, grad_normed):
    grad_f = grad_normed.astype(F32)
    inner = jnp.mean(grad_f * raw_rows, axis=-1, keepdims=True)
    return (factor * grad_f - raw_rows * factor * factor * factor * inner).astype(BF16)


def dot(a, b, dims):
    return lax.dot_general(a, b, (dims, ((), ())), preferred_element_type=F32)


def reduce_axis(blocks, axis, dim):
    place = (lax.axis_index("batch") // (16, 4, 1)[axis]) % 4
    total = pick(blocks, place, dim)
    for distance in (1, 2, 3):
        sent = pick(blocks, (place + distance) % 4, dim).astype(BF16)
        total = total + shift_batch(sent, axis, distance).astype(F32)
    return total


def first_stage(table):
    return reduce_axis(table[:2], 1, 1), reduce_axis(table[2:], 2, 2)


def shards(embedded, conv_weight, qkv_weight, cotangent):
    own = embedded[0]
    rows, channels = own.shape
    half = rows // 2
    length = 4 * rows
    seq = lax.axis_index("seq")
    core = seq % 2
    chip = seq // 2

    blocks = [own, swap_seq(own, 1), swap_seq(own, 2)]
    blocks.append(swap_seq(blocks[2], 1))
    window = jnp.zeros((length, channels), BF16)
    for mask in range(4):
        window = lax.dynamic_update_slice(window, blocks[mask], ((seq ^ mask) * rows, 0))

    grad_heads = cotangent[0].reshape(half, HEADS, HV).transpose(1, 0, 2)
    grad_in = jnp.zeros((4 * half, HV), BF16)
    for mask in range(4):
        piece = pick(grad_heads, seq ^ mask)
        if mask:
            piece = swap_seq(piece, mask)
        grad_in = lax.dynamic_update_slice(grad_in, piece, ((seq ^ mask) * half, 0))

    weight_heads = jnp.stack(
        [
            jnp.concatenate(
                [
                    qkv_weight[:, h * HK : (h + 1) * HK],
                    qkv_weight[:, (HEADS + h) * HK : (HEADS + h + 1) * HK],
                    qkv_weight[:, 2 * HEADS * HK + h * HV : 2 * HEADS * HK + (h + 1) * HV],
                ],
                axis=1,
            )
            for h in range(HEADS)
        ]
    )
    weight_own = pick(weight_heads, seq)

    activated = jax.nn.gelu(window.astype(F32), approximate=True).astype(BF16)
    padded = jnp.pad(activated, ((STEP, STEP), (0, 0)))
    stacked = jnp.concatenate([padded[t * STEP : t * STEP + length] for t in range(3)], axis=1)
    hidden = (window.astype(F32) + dot(stacked, conv_weight, ((1,), (0,)))).astype(BF16)
    joined = hidden.reshape(length // 2, 2 * channels)
    projected = dot(joined, weight_own, ((1,), (0,)))
    query_raw = projected[:, :HK]
    key_raw = projected[:, HK : 2 * HK]
    value = projected[:, 2 * HK :].astype(BF16)
    query, query_factor = normalize(query_raw)
    key, key_factor = normalize(key_raw)

    scores = dot(query, key, ((1,), (1,))) * temper
    expo = jnp.exp(scores)
    probs = expo / jnp.sum(expo, axis=-1, keepdims=True)
    probs_b = probs.astype(BF16)
    attended_head = dot(probs_b, value, ((1,), (0,))).astype(BF16)
    grad_value = dot(probs_b, grad_in, ((0,), (0,))).astype(BF16)
    grad_probs = dot(grad_in, value, ((1,), (1,)))
    inner = jnp.sum(probs * grad_probs, axis=-1, keepdims=True)
    grad_scores = (probs * (grad_probs - inner) * temper).astype(BF16)
    grad_query_n = dot(grad_scores, key, ((1,), (0,))).astype(BF16)
    grad_key_n = dot(grad_scores, query, ((0,), (0,))).astype(BF16)
    grad_query = normalize_back(query_raw, query_factor, grad_query_n)
    grad_key = normalize_back(key_raw, key_factor, grad_key_n)
    grad_head = jnp.concatenate([grad_query, grad_key, grad_value], axis=1)

    grad_chips = grad_head.reshape(2, 2 * half, HD)
    mine = pick(grad_chips, chip)
    theirs = swap_seq(pick(grad_chips, 1 - chip), 2)
    grad_proj = jnp.concatenate([mine, swap_seq(mine, 1), theirs, swap_seq(theirs, 1)], axis=1)

    qkv_table = dot(joined, grad_head, ((0,), (0,))).reshape(*GRID, -1, HD)
    qkv_x, qkv_y = first_stage(qkv_table)

    attended_parts = attended_head.reshape(4, half, HV)
    attended = jnp.zeros((HEADS, half, HV), BF16)
    for mask in range(4):
        piece = pick(attended_parts, seq ^ mask)
        if mask:
            piece = swap_seq(piece, mask)
        attended = lax.dynamic_update_slice(attended, piece[None], (seq ^ mask, 0, 0))
    attended = attended.transpose(1, 0, 2).reshape(1, half, HEADS * HV)

    width = channels // 2
    weight_rows = jnp.concatenate(
        [pick(weight_heads, seq ^ mask) for mask in range(4)], axis=1
    ).reshape(2, 2, width, HEADS * HD)
    weight_back = pick(weight_rows, core, 1).reshape(channels, HEADS * HD)
    grad_hidden = dot(grad_proj, weight_back, ((1,), (1,))).astype(BF16)
    grad_bins = grad_hidden.reshape(2 * rows, width)
    stacked_chip = lax.dynamic_slice(stacked, (chip * 2 * rows, 0), (2 * rows, 3 * channels))
    conv_table = dot(stacked_chip, grad_bins, ((0,), (0,))).reshape(*GRID, -1, width)
    conv_x, conv_y = first_stage(conv_table)

    totals = []
    for part_x, part_y in ((conv_x, conv_y), (qkv_x, qkv_y)):
        done = jnp.concatenate([reduce_axis(part_x, 2, 1), reduce_axis(part_y, 1, 1)])
        totals.append(reduce_axis(done, 0, 0).astype(BF16))
    conv_own, qkv_own = totals
    conv_parts = [conv_own] + [swap_seq(conv_own, mask) for mask in (1, 2, 3)]
    qkv_parts = [qkv_own] + [swap_seq(qkv_own, mask) for mask in (1, 2, 3)]
    conv_here = conv_parts[0].astype(F32) + conv_parts[2].astype(F32)
    conv_there = conv_parts[1].astype(F32) + conv_parts[3].astype(F32)
    conv_pair = jnp.stack([conv_here, conv_there])
    grad_conv = jnp.concatenate([pick(conv_pair, core), pick(conv_pair, 1 - core)], axis=1)
    qkv_stack = jnp.stack(qkv_parts).astype(F32)
    heads = [pick(qkv_stack, seq ^ h) for h in range(HEADS)]
    grad_qkv = jnp.concatenate(
        [h[:, :HK] for h in heads]
        + [h[:, HK : 2 * HK] for h in heads]
        + [h[:, 2 * HK :] for h in heads],
        axis=1,
    )
    return attended, grad_conv, grad_qkv


def solution(mesh):
    return jax.shard_map(
        shards,
        mesh=mesh,
        in_specs=(P("batch", "seq", None), P(), P(), P("batch", "seq", None)),
        out_specs=(P("batch", "seq", None), P("batch", None), P("batch", None)),
        check_vma=False,
    )
```

```python
import math

import jax
import jax.numpy as jnp
from jax import lax
from jax.experimental import pallas as pl
from jax.experimental.pallas import tpu as pltpu
from jax.sharding import PartitionSpec as P

HEADS = 4
HK = 128
HV = 192
WIN = 256
HD = 2 * HK + WIN
STEP = 4
C = 768
BINS = 512
PAIRS = 256
CHIP = 512
PAD = 8
CR = 36
QR = 24
QOFF = 112
JR = QOFF + 4 * QR
F32 = jnp.float32
BF16 = jnp.bfloat16

epsilon = 1e-06
temper = 1.0 / math.sqrt(HK)

VMEM = pl.BlockSpec(memory_space=pltpu.VMEM)
SMEM = pl.BlockSpec(memory_space=pltpu.SMEM)


def params(mib=48):
    return pltpu.CompilerParams(vmem_limit_bytes=mib << 20)


def shape(dims, dtype=BF16):
    return jax.ShapeDtypeStruct(dims, dtype)


def cost(flops, nbytes):
    return pl.CostEstimate(flops=flops, bytes_accessed=nbytes, transcendentals=0)


def dot(a, b, ca=1, cb=0):
    return lax.dot_general(a, b, (((ca,), (cb,)), ((), ())), preferred_element_type=F32)


def swap_seq(block, mask):
    return lax.ppermute(block, "seq", [(i, i ^ mask) for i in range(4)])


def shift_batch(block, axis, distance):
    pairs = []
    for b in range(64):
        place = [b // 16, (b // 4) % 4, b % 4]
        place[axis] = (place[axis] + distance) % 4
        pairs.append((b, place[0] * 16 + place[1] * 4 + place[2]))
    return lax.ppermute(block, "batch", pairs)


def conv_kernel(where, first, second, low, high, taps, wq, wk, wv0, wv1, act, joined, proj, bins):
    core = where[1]
    for j in range(6):
        span = slice(j * 128, (j + 1) * 128)
        bins[j, 0:8, :] = low[:, span]
        here = pl.multiple_of(8 + core * BINS, 8)
        bins[j, pl.ds(here, BINS), :] = first[:, span].astype(F32)
        here = pl.multiple_of(8 + (1 - core) * BINS, 8)
        bins[j, pl.ds(here, BINS), :] = second[:, span].astype(F32)
        bins[j, 8 + 2 * BINS :, :] = high[:, span]

    def stream(parity, start, count):
        place = 8 + 2 * start + parity
        return jnp.concatenate(
            [bins[j, pl.ds(place, count, stride=2), :] for j in range(6)], axis=1
        )

    tile = 256
    for parity in range(2):
        for start, count in ((-4, 4), (0, tile), (tile, tile), (CHIP, 4)):
            act[parity, PAD + start : PAD + start + count, :] = jax.nn.gelu(
                stream(parity, start, count), approximate=True
            )
    for row in range(0, CHIP, tile):
        for parity in range(2):
            out = stream(parity, row, tile)
            for tap in range(3):
                start = PAD + row + (tap - 1) * (STEP // 2)
                out = out + dot(
                    act[parity, start : start + tile, :].astype(BF16),
                    taps[tap * C : (tap + 1) * C, :],
                )
            hidden = out.astype(BF16)
            joined[row : row + tile, parity * C : (parity + 1) * C] = hidden
            for column, weight in enumerate((wq, wk, wv0, wv1)):
                span = slice(column * HK, (column + 1) * HK)
                part = dot(hidden, weight[parity * C : (parity + 1) * C, :])
                if parity:
                    proj[row : row + tile, span] += part
                else:
                    proj[row : row + tile, span] = part


def conv_chip(where, first, second, low, high, taps, weight):
    full = lambda dims: pl.BlockSpec(dims, lambda i, w: (0,) * len(dims))
    column = lambda f: pl.BlockSpec((2 * C, HK), lambda i, w: (0, f(w[0])))
    return pl.pallas_call(
        conv_kernel,
        grid_spec=pltpu.PrefetchScalarGridSpec(
            num_scalar_prefetch=1,
            grid=(1,),
            in_specs=[
                full((BINS, C)),
                full((BINS, C)),
                full((8, C)),
                full((8, C)),
                full((3 * C, C)),
                column(lambda s: s),
                column(lambda s: HEADS + s),
                column(lambda s: 2 * HEADS + (3 * s) // 2),
                column(lambda s: 2 * HEADS + (3 * s) // 2 + 1),
            ],
            out_specs=[
                full((2, CHIP + 2 * PAD, C)),
                full((CHIP, 2 * C)),
                full((CHIP, HD)),
            ],
            scratch_shapes=[pltpu.VMEM((6, 2 * BINS + 16, 128), F32)],
        ),
        out_shape=[
            shape((2, CHIP + 2 * PAD, C), F32),
            shape((CHIP, 2 * C)),
            shape((CHIP, HD), F32),
        ],
        compiler_params=params(),
        cost_estimate=cost(2 * 1024 * 3 * C * C + 2 * CHIP * 2 * C * HD, 12 << 20),
        name="conv_chip",
    )(where, first, second, low, high, taps, weight, weight, weight, weight)


def unit(raw):
    return lax.rsqrt(jnp.mean(raw * raw, axis=-1, keepdims=True) + epsilon)


def unit_back(raw, grad_normed):
    factor = unit(raw)
    grad_f = grad_normed.astype(F32)
    inner = jnp.mean(grad_f * raw, axis=-1, keepdims=True)
    return (factor * grad_f - raw * factor * factor * factor * inner).astype(BF16)


def attention_kernel(
    where, proj_a, proj_b, g0, g1, g2, g3, grad_a, grad_b, att_mine, att_side, att_b,
    query, key, value, grad, key_sum, value_sum,
):
    core = where[1]
    lane = lax.broadcasted_iota(jnp.int32, (CHIP, WIN), 1)
    valid = (lane >= 64 * core) & (lane < 64 * core + HV)
    for part, proj in enumerate((proj_a, proj_b)):
        rows = slice(part * CHIP, (part + 1) * CHIP)
        raw = proj[:, :HK]
        query[rows, :] = (raw * unit(raw)).astype(BF16)
        raw = proj[:, HK : 2 * HK]
        key[rows, :] = (raw * unit(raw)).astype(BF16)
        value[rows, :] = jnp.where(valid, proj[:, 2 * HK :], 0.0).astype(BF16)
    for part, pair in enumerate(((g0, g1), (g2, g3))):
        for side in range(2):
            place = pl.multiple_of(part * CHIP + (core ^ side) * PAIRS, PAIRS)
            grad[pl.ds(place, PAIRS), :] = pair[side][...]
    keys, values = key[...], value[...]
    for tile in range(4):
        rows = slice(tile * PAIRS, (tile + 1) * PAIRS)
        local = slice((tile % 2) * PAIRS, (tile % 2 + 1) * PAIRS)
        queries, grads = query[rows, :], grad[rows, :]
        expo = jnp.exp(dot(queries, keys, 1, 1) * temper)
        probs = expo * (1.0 / jnp.sum(expo, axis=-1, keepdims=True))
        probs_b = probs.astype(BF16)
        attended = dot(probs_b, values).astype(BF16)
        if tile < 2:

            @pl.when(core == tile)
            def _():
                att_mine[...] = attended

            @pl.when(core != tile)
            def _():
                att_side[...] = attended
        else:
            att_b[core ^ (tile - 2)] = attended
        grad_value = dot(probs_b, grads, 0, 0)
        grad_probs = dot(grads, values, 1, 1)
        inner = jnp.sum(probs * grad_probs, axis=-1, keepdims=True)
        grad_scores = (probs * (grad_probs - inner) * temper).astype(BF16)
        grad_query = dot(grad_scores, keys).astype(BF16)
        grad_key = dot(grad_scores, queries, 0, 0)
        if tile:
            value_sum[...] += grad_value
            key_sum[...] += grad_key
        else:
            value_sum[...] = grad_value
            key_sum[...] = grad_key
        proj, out = (proj_a, grad_a) if tile < 2 else (proj_b, grad_b)
        out[local, :HK] = unit_back(proj[local, :HK], grad_query)
    for part, (proj, out) in enumerate(((proj_a, grad_a), (proj_b, grad_b))):
        rows = slice(part * CHIP, (part + 1) * CHIP)
        out[:, HK : 2 * HK] = unit_back(proj[:, HK : 2 * HK], key_sum[rows, :].astype(BF16))
        out[:, 2 * HK :] = jnp.where(valid, value_sum[rows, :], 0.0).astype(BF16)


def attention(where, proj_a, proj_b, grads):
    return pl.pallas_call(
        attention_kernel,
        in_specs=[SMEM] + [VMEM] * 6,
        out_specs=[VMEM] * 5,
        out_shape=[
            shape((CHIP, HD)),
            shape((CHIP, HD)),
            shape((PAIRS, WIN)),
            shape((PAIRS, WIN)),
            shape((2, PAIRS, WIN)),
        ],
        scratch_shapes=[
            pltpu.VMEM((2 * CHIP, HK), BF16),
            pltpu.VMEM((2 * CHIP, HK), BF16),
            pltpu.VMEM((2 * CHIP, WIN), BF16),
            pltpu.VMEM((2 * CHIP, WIN), BF16),
            pltpu.VMEM((2 * CHIP, HK), F32),
            pltpu.VMEM((2 * CHIP, WIN), F32),
        ],
        compiler_params=params(),
        cost_estimate=cost(6 * 2 * 1024 * 1024 * 192, 6 << 20),
        name="attention",
    )(where, proj_a, proj_b, *grads)


def qkv_kernel(where, joined_a, joined_b, grad_a, grad_b, *refs):
    out_x, out_y, table = refs[:4], refs[4:8], refs[8]
    x, y = where[3], where[4]
    block = 4 * QR
    for zh in range(4):
        columns = slice(zh * 4 * block, (zh + 1) * 4 * block)
        table[...] = dot(joined_a[:, columns], grad_a[...], 0, 0) + dot(
            joined_b[:, columns], grad_b[...], 0, 0
        )
        for d in range(4):
            if zh < 2:
                start = pl.multiple_of(((x + d) % 4) * block, 8)
                out_x[d][zh] = table[pl.ds(start, block), :].astype(BF16)
            else:
                for xx in range(4):
                    start = pl.multiple_of(xx * block + ((y + d) % 4) * QR, 8)
                    out_y[d][zh - 2, xx * QR : (xx + 1) * QR, :] = table[
                        pl.ds(start, QR), :
                    ].astype(BF16)


def qkv_gradient(where, joined_a, joined_b, grad_a, grad_b):
    return pl.pallas_call(
        qkv_kernel,
        in_specs=[SMEM] + [VMEM] * 4,
        out_specs=[VMEM] * 8,
        out_shape=[shape((2, 4 * QR, HD))] * 8,
        scratch_shapes=[pltpu.VMEM((16 * QR, HD), F32)],
        compiler_params=params(),
        cost_estimate=cost(2 * 1536 * 1024 * HD, 6 << 20),
        name="qkv_gradient",
    )(where, joined_a, joined_b, grad_a, grad_b)


def value_units(place, heads):
    place(0, heads[0][0])
    place(1, heads[0][1] + heads[1][0])
    place(2, heads[1][1])
    place(3, heads[2][0])
    place(4, heads[2][1] + heads[3][0])
    place(5, heads[3][1])


def conv_gradient_kernel(where, g0, g1, g2, g3, even, odd, act, *refs):
    out_x, out_y = refs[:4], refs[4:8]
    by_head, natural, table, pieces = refs[8:]
    seq, x, y = where[0], where[3], where[4]
    for mask, ref in enumerate((g0, g1, g2, g3)):
        by_head[seq ^ mask] = ref[...]
    for h in range(HEADS):
        natural[:, h * HK : (h + 1) * HK] = by_head[h, :, :HK]
        natural[:, (HEADS + h) * HK : (HEADS + h + 1) * HK] = by_head[h, :, HK : 2 * HK]

    def place(index, rows):
        natural[:, (2 * HEADS + index) * HK : (2 * HEADS + index + 1) * HK] = rows

    value_units(
        place, [[by_head[h, :, (2 + k) * HK : (3 + k) * HK] for k in range(2)] for h in range(HEADS)]
    )
    rows = natural[...]
    hidden = [dot(rows, weight[...], 1, 1).astype(BF16) for weight in (even, odd)]
    for tap in range(3):
        start = PAD + (tap - 1) * (STEP // 2)
        for part in range(2):
            span = slice(part * 384, (part + 1) * 384)
            out = slice(tap * C + part * 384, tap * C + (part + 1) * 384)
            table[out, :] = dot(
                act[0, start : start + CHIP, span].astype(BF16), hidden[0], 0, 0
            ) + dot(act[1, start : start + CHIP, span].astype(BF16), hidden[1], 0, 0)
    block = 4 * CR
    for zh in range(2):
        for d in range(4):
            begin = pl.multiple_of((4 * zh + (x + d) % 4) * block, 8)
            out_x[d][zh] = table[pl.ds(begin, block), :].astype(BF16)
        for xx in range(4):
            chunk = table[(8 + 4 * zh + xx) * block : (9 + 4 * zh + xx) * block, :]
            for yy in range(4):
                pieces[(yy - y + 4) % 4, zh, xx * CR : (xx + 1) * CR, :] = chunk[
                    yy * CR : (yy + 1) * CR, :
                ]
    for d in range(4):
        out_y[d][...] = pieces[d].astype(BF16)


def conv_gradient(where, grads, weight, act):
    full = lambda dims: pl.BlockSpec(dims, lambda i, w: (0,) * len(dims))
    return pl.pallas_call(
        conv_gradient_kernel,
        grid_spec=pltpu.PrefetchScalarGridSpec(
            num_scalar_prefetch=1,
            grid=(1,),
            in_specs=[full((CHIP, HD))] * 4
            + [
                pl.BlockSpec((C // 2, 1792), lambda i, w: (w[1], 0)),
                pl.BlockSpec((C // 2, 1792), lambda i, w: (2 + w[1], 0)),
                full((2, CHIP + 2 * PAD, C)),
            ],
            out_specs=[full((2, 4 * CR, C // 2))] * 8,
            scratch_shapes=[
                pltpu.VMEM((HEADS, CHIP, HD), BF16),
                pltpu.VMEM((CHIP, 1792), BF16),
                pltpu.VMEM((3 * C, C // 2), F32),
                pltpu.VMEM((4, 2, 4 * CR, C // 2), F32),
            ],
        ),
        out_shape=[shape((2, 4 * CR, C // 2))] * 8,
        compiler_params=params(),
        cost_estimate=cost(2 * CHIP * 1792 * C + 2 * 1024 * 3 * C * C // 2, 10 << 20),
        name="conv_gradient",
    )(where, *grads, weight, weight, act)


def total(refs):
    out = refs[0][...].astype(F32)
    for ref in refs[1:]:
        out = out + ref[...].astype(F32)
    return out


def second_kernel(where, *refs):
    conv_x, conv_y, qkv_x, qkv_y = (refs[4 * i : 4 * i + 4] for i in range(4))
    outs, pieces = refs[16:24], refs[24]
    for half, (conv, qkv, me) in enumerate(
        ((conv_x, qkv_x, where[4]), (conv_y, qkv_y, where[3]))
    ):
        conv_sum, qkv_sum = total(conv), total(qkv)
        for zh in range(2):
            for k in range(4):
                d = (k - me + 4) % 4
                for j in range(3):
                    pieces[d, zh, j * CR : (j + 1) * CR, :] = conv_sum[
                        zh, k * CR : (k + 1) * CR, j * 128 : (j + 1) * 128
                    ]
                pieces[d, zh, 3 * CR : QOFF, :] = jnp.zeros((QOFF - 3 * CR, 128), F32)
                for j in range(4):
                    pieces[d, zh, QOFF + j * QR : QOFF + (j + 1) * QR, :] = qkv_sum[
                        zh, k * QR : (k + 1) * QR, j * 128 : (j + 1) * 128
                    ]
        for d in range(4):
            outs[4 * half + d][...] = pieces[d].astype(BF16)


def second_stage(where, *blocks):
    return pl.pallas_call(
        second_kernel,
        in_specs=[SMEM] + [VMEM] * 16,
        out_specs=[VMEM] * 8,
        out_shape=[shape((2, JR, 128))] * 8,
        scratch_shapes=[pltpu.VMEM((4, 2, JR, 128), F32)],
        compiler_params=params(),
        name="second_stage",
    )(where, *blocks)


def third_kernel(where, *refs):
    outs, sums = refs[8:12], refs[12]
    sums[0:2] = total(refs[0:4])
    sums[2:4] = total(refs[4:8])
    for d in range(4):
        outs[d][...] = sums[(where[2] + d) % 4].astype(BF16)


def third_stage(where, *blocks):
    return pl.pallas_call(
        third_kernel,
        in_specs=[SMEM] + [VMEM] * 8,
        out_specs=[VMEM] * 4,
        out_shape=[shape((JR, 128))] * 4,
        scratch_shapes=[pltpu.VMEM((4, JR, 128), F32)],
        compiler_params=params(),
        name="third_stage",
    )(where, *blocks)


def last_kernel(where, r0, r1, r2, r3, grad_conv, grad_qkv, by_head):
    seq, core = where[0], where[1]
    parts = [ref[...].astype(F32) for ref in (r0, r1, r2, r3)]
    here = parts[0] + parts[2]
    there = parts[1] + parts[3]
    low = jnp.where(core == 0, here, there)
    high = jnp.where(core == 0, there, here)
    for j in range(3):
        span = slice(j * CR, (j + 1) * CR)
        grad_conv[:, j * 128 : (j + 1) * 128] = low[span, :]
        grad_conv[:, (3 + j) * 128 : (4 + j) * 128] = high[span, :]
    for mask in range(4):
        by_head[seq ^ mask] = parts[mask][QOFF:, :]

    def place(index, rows):
        grad_qkv[:, index * 128 : (index + 1) * 128] = rows

    for h in range(HEADS):
        place(h, by_head[h, :QR, :])
        place(HEADS + h, by_head[h, QR : 2 * QR, :])
    value_units(
        lambda index, rows: place(2 * HEADS + index, rows),
        [[by_head[h, (2 + k) * QR : (3 + k) * QR, :] for k in range(2)] for h in range(HEADS)],
    )


def last_stage(where, parts):
    return pl.pallas_call(
        last_kernel,
        in_specs=[SMEM] + [VMEM] * 4,
        out_specs=[VMEM] * 2,
        out_shape=[shape((CR, C), F32), shape((QR, 1792), F32)],
        scratch_shapes=[pltpu.VMEM((HEADS, 4 * QR, 128), F32)],
        compiler_params=params(),
        name="last_stage",
    )(where, *parts)


def attended_kernel(where, a0, a1, a2, a3, out, by_head):
    for mask, ref in enumerate((a0, a1, a2, a3)):
        by_head[where[0] ^ mask] = ref[...]

    def place(index, rows):
        out[:, index * 128 : (index + 1) * 128] = rows

    value_units(
        place, [[by_head[h, :, k * HK : (k + 1) * HK] for k in range(2)] for h in range(HEADS)]
    )


def attended_rows(where, parts):
    return pl.pallas_call(
        attended_kernel,
        in_specs=[SMEM] + [VMEM] * 4,
        out_specs=VMEM,
        out_shape=shape((PAIRS, C)),
        scratch_shapes=[pltpu.VMEM((HEADS, PAIRS, WIN), BF16)],
        compiler_params=params(),
        name="attended_rows",
    )(where, *parts)


def shards(embedded, conv_weight, qkv_weight, cotangent):
    own = embedded[0]
    seq = lax.axis_index("seq")
    batch = lax.axis_index("batch")
    core, chip = seq % 2, seq // 2
    where = jnp.stack([seq, core, batch // 16, (batch // 4) % 4, batch % 4]).astype(jnp.int32)

    edges = jnp.concatenate([own[:8], own[-8:]])
    edge_same, edge_other = swap_seq(edges, 2), swap_seq(edges, 3)
    side = swap_seq(own, 1)
    far = swap_seq(own, 2)
    far_side = swap_seq(far, 1)
    zero = jnp.zeros((8, C), F32)
    first = lambda a, b: jnp.where(core == 0, a, b)[:8].astype(F32)
    last = lambda a, b: jnp.where(core == 0, b, a)[8:].astype(F32)
    side_edges = jnp.concatenate([side[:8], side[-8:]])
    own_low = jnp.where(chip == 1, last(edge_same, edge_other), zero)
    own_high = jnp.where(chip == 0, first(edge_same, edge_other), zero)
    far_low = jnp.where(chip == 0, last(edges, side_edges), zero)
    far_high = jnp.where(chip == 1, first(edges, side_edges), zero)

    grads = []
    for mask in range(4):
        head = seq ^ mask
        piece = lax.dynamic_slice(cotangent[0], (0, ((3 * head) // 2) * HK), (PAIRS, WIN))
        grads.append(swap_seq(piece, mask) if mask else piece)

    act, joined_a, proj_a = conv_chip(where, own, side, own_low, own_high, conv_weight, qkv_weight)
    _, joined_b, proj_b = conv_chip(where, far, far_side, far_low, far_high, conv_weight, qkv_weight)

    grad_a, grad_b, att_mine, att_side, att_b = attention(where, proj_a, proj_b, grads)

    far_grad = swap_seq(grad_b, 2)
    side_grad = swap_seq(grad_a, 1)
    far_side_grad = swap_seq(far_grad, 1)
    att_far = swap_seq(att_b, 2)
    attended = attended_rows(
        where, (att_mine, swap_seq(att_side, 1), att_far[0], swap_seq(att_far[1], 1))
    )

    def sent(blocks, axis):
        return [blocks[0]] + [shift_batch(blocks[d], axis, d) for d in (1, 2, 3)]

    qkv_blocks = qkv_gradient(where, joined_a, joined_b, grad_a, grad_b)
    qkv_x, qkv_y = sent(qkv_blocks[:4], 1), sent(qkv_blocks[4:], 2)
    conv_blocks = conv_gradient(
        where, (grad_a, side_grad, far_grad, far_side_grad), qkv_weight, act
    )
    conv_x, conv_y = sent(conv_blocks[:4], 1), sent(conv_blocks[4:], 2)

    blocks = second_stage(where, *conv_x, *conv_y, *qkv_x, *qkv_y)
    blocks = third_stage(where, *sent(blocks[:4], 2), *sent(blocks[4:], 1))
    parts = sent(blocks, 0)
    summed = sum(part.astype(F32) for part in parts).astype(BF16)
    grad_conv, grad_qkv = last_stage(
        where, [summed] + [swap_seq(summed, mask) for mask in (1, 2, 3)]
    )
    return attended.reshape(1, PAIRS, HEADS * HV), grad_conv, grad_qkv


def solution(mesh):
    return jax.shard_map(
        shards,
        mesh=mesh,
        in_specs=(P("batch", "seq", None), P(), P(), P("batch", "seq", None)),
        out_specs=(P("batch", "seq", None), P("batch", None), P("batch", None)),
        check_vma=False,
    )
```

```python
import functools
import math

import jax
import jax.numpy as jnp
from jax import lax
from jax.experimental import pallas as pl
from jax.experimental.pallas import tpu as pltpu
from jax.sharding import PartitionSpec as P

HEADS = 4
HK = 128
HV = 192
WIN = 256
HD = 2 * HK + WIN
STEP = 4
C = 768
BINS = 512
PAIRS = 256
CHIP = 512
PAD = 8
CR = 36
QR = 24
F32 = jnp.float32
BF16 = jnp.bfloat16

epsilon = 1e-06
temper = 1.0 / math.sqrt(HK)

VMEM = pl.BlockSpec(memory_space=pltpu.VMEM)
SMEM = pl.BlockSpec(memory_space=pltpu.SMEM)


def params(mib=48):
    return pltpu.CompilerParams(vmem_limit_bytes=mib << 20)


def shape(dims, dtype=BF16):
    return jax.ShapeDtypeStruct(dims, dtype)


def cost(flops, nbytes):
    return pl.CostEstimate(flops=flops, bytes_accessed=nbytes, transcendentals=0)


def dot(a, b, ca=1, cb=0):
    return lax.dot_general(a, b, (((ca,), (cb,)), ((), ())), preferred_element_type=F32)


def swap_seq(block, mask):
    return lax.ppermute(block, "seq", [(i, i ^ mask) for i in range(4)])


def shift_batch(block, axis, distance):
    pairs = []
    for b in range(64):
        place = [b // 16, (b // 4) % 4, b % 4]
        place[axis] = (place[axis] + distance) % 4
        pairs.append((b, place[0] * 16 + place[1] * 4 + place[2]))
    return lax.ppermute(block, "batch", pairs)


def over_plane(blocks):
    groups = [[zh * 16 + place for place in range(16)] for zh in range(4)]
    return lax.all_to_all(
        blocks, "batch", split_axis=0, concat_axis=0, axis_index_groups=groups, tiled=True
    )


def conv_kernel(keep, where, first, second, low, high, taps, weight, joined, proj, *refs):
    columns = refs[0] if keep else None
    act, stacked, bins = refs[-3:]
    core = where[1]
    for j in range(6):
        span = slice(j * 128, (j + 1) * 128)
        bins[j, 0:8, :] = low[:, span]
        here = pl.multiple_of(8 + core * BINS, 8)
        bins[j, pl.ds(here, BINS), :] = first[:, span].astype(F32)
        here = pl.multiple_of(8 + (1 - core) * BINS, 8)
        bins[j, pl.ds(here, BINS), :] = second[:, span].astype(F32)
        bins[j, 8 + 2 * BINS :, :] = high[:, span]

    def stream(parity, start, count):
        place = 8 + 2 * start + parity
        return jnp.concatenate(
            [bins[j, pl.ds(place, count, stride=2), :] for j in range(6)], axis=1
        )

    for parity in range(2):
        for start, count in ((-4, 4), (0, CHIP), (CHIP, 4)):
            act[PAD + start : PAD + start + count, :] = jax.nn.gelu(
                stream(parity, start, count), approximate=True
            )
        for tap in range(3):
            start = PAD + (tap - 1) * (STEP // 2)
            rows = act[start : start + CHIP, :].astype(BF16)
            stacked[:, tap * C : (tap + 1) * C] = rows
            if keep:
                columns[parity, tap * C : (tap + 1) * C, :] = rows.T
        out = stream(parity, 0, CHIP) + dot(stacked[...], taps[...])
        joined[:, parity * C : (parity + 1) * C] = out.astype(BF16)
    proj[...] = dot(joined[...], weight[...])


def conv_chip(keep, where, first, second, low, high, taps, weight):
    return pl.pallas_call(
        functools.partial(conv_kernel, keep),
        in_specs=[SMEM] + [VMEM] * 6,
        out_specs=[VMEM] * (3 if keep else 2),
        out_shape=[shape((CHIP, 2 * C)), shape((CHIP, HD), F32)]
        + ([shape((2, 3 * C, CHIP))] if keep else []),
        scratch_shapes=[
            pltpu.VMEM((CHIP + 2 * PAD, C), F32),
            pltpu.VMEM((CHIP, 3 * C), BF16),
            pltpu.VMEM((6, 2 * BINS + 16, 128), F32),
        ],
        compiler_params=params(),
        cost_estimate=cost(2 * 1024 * 3 * C * C + 2 * CHIP * 2 * C * HD, 12 << 20),
        name="conv_own" if keep else "conv_far",
    )(where, first, second, low, high, taps, weight)


def unit(raw):
    return lax.rsqrt(jnp.mean(raw * raw, axis=-1, keepdims=True) + epsilon)


def unit_back(raw, grad_normed):
    factor = unit(raw)
    grad_f = grad_normed.astype(F32)
    inner = jnp.mean(grad_f * raw, axis=-1, keepdims=True)
    return (factor * grad_f - raw * factor * factor * factor * inner).astype(BF16)


def attention_kernel(
    where, proj_a, proj_b, g0, g1, g2, g3, grad_a, grad_b, att_mine, att_side, att_b,
    query, key, value, grad, key_sum, value_sum,
):
    core = where[1]
    lane = lax.broadcasted_iota(jnp.int32, (CHIP, WIN), 1)
    valid = (lane >= 64 * core) & (lane < 64 * core + HV)
    for part, proj in enumerate((proj_a, proj_b)):
        rows = slice(part * CHIP, (part + 1) * CHIP)
        raw = proj[:, :HK]
        query[rows, :] = (raw * unit(raw)).astype(BF16)
        raw = proj[:, HK : 2 * HK]
        key[rows, :] = (raw * unit(raw)).astype(BF16)
        value[rows, :] = jnp.where(valid, proj[:, 2 * HK :], 0.0).astype(BF16)
    for part, pair in enumerate(((g0, g1), (g2, g3))):
        for side in range(2):
            place = pl.multiple_of(part * CHIP + (core ^ side) * PAIRS, PAIRS)
            grad[pl.ds(place, PAIRS), :] = pair[side][...]
    keys, values = key[...], value[...]
    for tile in range(4):
        rows = slice(tile * PAIRS, (tile + 1) * PAIRS)
        local = slice((tile % 2) * PAIRS, (tile % 2 + 1) * PAIRS)
        queries, grads = query[rows, :], grad[rows, :]
        expo = jnp.exp(dot(queries, keys, 1, 1) * temper)
        probs = expo * (1.0 / jnp.sum(expo, axis=-1, keepdims=True))
        probs_b = probs.astype(BF16)
        attended = dot(probs_b, values).astype(BF16)
        if tile < 2:

            @pl.when(core == tile)
            def _():
                att_mine[...] = attended

            @pl.when(core != tile)
            def _():
                att_side[...] = attended
        else:
            att_b[core ^ (tile - 2)] = attended
        grad_value = dot(probs_b, grads, 0, 0)
        grad_probs = dot(grads, values, 1, 1)
        inner = jnp.sum(probs * grad_probs, axis=-1, keepdims=True)
        grad_scores = (probs * (grad_probs - inner) * temper).astype(BF16)
        grad_query = dot(grad_scores, keys).astype(BF16)
        grad_key = dot(grad_scores, queries, 0, 0)
        if tile:
            value_sum[...] += grad_value
            key_sum[...] += grad_key
        else:
            value_sum[...] = grad_value
            key_sum[...] = grad_key
        proj, out = (proj_a, grad_a) if tile < 2 else (proj_b, grad_b)
        out[local, :HK] = unit_back(proj[local, :HK], grad_query)
    for part, (proj, out) in enumerate(((proj_a, grad_a), (proj_b, grad_b))):
        rows = slice(part * CHIP, (part + 1) * CHIP)
        out[:, HK : 2 * HK] = unit_back(proj[:, HK : 2 * HK], key_sum[rows, :].astype(BF16))
        out[:, 2 * HK :] = jnp.where(valid, value_sum[rows, :], 0.0).astype(BF16)


def attention(where, proj_a, proj_b, grads):
    return pl.pallas_call(
        attention_kernel,
        in_specs=[SMEM] + [VMEM] * 6,
        out_specs=[VMEM] * 5,
        out_shape=[
            shape((CHIP, HD)),
            shape((CHIP, HD)),
            shape((PAIRS, WIN)),
            shape((PAIRS, WIN)),
            shape((2, PAIRS, WIN)),
        ],
        scratch_shapes=[
            pltpu.VMEM((2 * CHIP, HK), BF16),
            pltpu.VMEM((2 * CHIP, HK), BF16),
            pltpu.VMEM((2 * CHIP, WIN), BF16),
            pltpu.VMEM((2 * CHIP, WIN), BF16),
            pltpu.VMEM((2 * CHIP, HK), F32),
            pltpu.VMEM((2 * CHIP, WIN), F32),
        ],
        compiler_params=params(),
        cost_estimate=cost(6 * 2 * 1024 * 1024 * 192, 6 << 20),
        name="attention",
    )(where, proj_a, proj_b, *grads)


def qkv_kernel(joined_a, joined_b, grad_a, grad_b, out):
    for zh in range(4):
        columns = slice(zh * 16 * QR, (zh + 1) * 16 * QR)
        table = dot(joined_a[:, columns], grad_a[...], 0, 0) + dot(
            joined_b[:, columns], grad_b[...], 0, 0
        )
        for place in range(16):
            out[place, zh * QR : (zh + 1) * QR, :] = table[
                place * QR : (place + 1) * QR, :
            ].astype(BF16)


def qkv_gradient(joined_a, joined_b, grad_a, grad_b):
    return pl.pallas_call(
        qkv_kernel,
        in_specs=[VMEM] * 4,
        out_specs=VMEM,
        out_shape=shape((16, 4 * QR, HD)),
        compiler_params=params(),
        cost_estimate=cost(2 * 1536 * 1024 * HD, 6 << 20),
        name="qkv_gradient",
    )(joined_a, joined_b, grad_a, grad_b)


def value_units(place, heads):
    place(0, heads[0][0])
    place(1, heads[0][1] + heads[1][0])
    place(2, heads[1][1])
    place(3, heads[2][0])
    place(4, heads[2][1] + heads[3][0])
    place(5, heads[3][1])


def conv_gradient_kernel(where, g0, g1, g2, g3, weight, columns, out, by_head, natural):
    seq = where[0]
    for mask, ref in enumerate((g0, g1, g2, g3)):
        by_head[seq ^ mask] = ref[...]
    for h in range(HEADS):
        natural[:, h * HK : (h + 1) * HK] = by_head[h, :, :HK]
        natural[:, (HEADS + h) * HK : (HEADS + h + 1) * HK] = by_head[h, :, HK : 2 * HK]

    def place(index, rows):
        natural[:, (2 * HEADS + index) * HK : (2 * HEADS + index + 1) * HK] = rows

    value_units(
        place, [[by_head[h, :, (2 + k) * HK : (3 + k) * HK] for k in range(2)] for h in range(HEADS)]
    )
    hidden = dot(natural[...], weight[...], 1, 1).astype(BF16)
    for zh in range(4):
        rows = slice(zh * 16 * CR, (zh + 1) * 16 * CR)
        table = dot(columns[0, rows, :], hidden[:, : C // 2]) + dot(
            columns[1, rows, :], hidden[:, C // 2 :]
        )
        for block in range(16):
            out[block, zh * CR : (zh + 1) * CR, :] = table[
                block * CR : (block + 1) * CR, :
            ].astype(BF16)


def conv_gradient(where, grads, weight, columns):
    return pl.pallas_call(
        conv_gradient_kernel,
        in_specs=[SMEM] + [VMEM] * 6,
        out_specs=VMEM,
        out_shape=shape((16, 4 * CR, C // 2)),
        scratch_shapes=[
            pltpu.VMEM((HEADS, CHIP, HD), BF16),
            pltpu.VMEM((CHIP, 1792), BF16),
        ],
        compiler_params=params(),
        cost_estimate=cost(2 * CHIP * 1792 * C + 2 * 1024 * 3 * C * C // 2, 10 << 20),
        name="conv_gradient",
    )(where, *grads, weight, columns)


def sum_kernel(where, blocks, *refs):
    outs, sums = refs[:4], refs[4]
    out = blocks[0].astype(F32)
    for place in range(1, 16):
        out = out + blocks[place].astype(F32)
    rows = sums.shape[1]
    for zh in range(4):
        sums[zh] = out[zh * rows : (zh + 1) * rows, :]
    for d in range(4):
        outs[d][...] = sums[(where[2] + d) % 4].astype(BF16)


def sum_stage(where, blocks):
    dims = (blocks.shape[1] // 4, blocks.shape[2])
    return pl.pallas_call(
        sum_kernel,
        in_specs=[SMEM, VMEM],
        out_specs=[VMEM] * 4,
        out_shape=[shape(dims)] * 4,
        scratch_shapes=[pltpu.VMEM((4, *dims), F32)],
        compiler_params=params(),
        name="sum_stage",
    )(where, blocks)


def last_conv_kernel(where, r0, r1, r2, r3, grad_conv):
    core = where[1]
    here = r0[...].astype(F32) + r2[...].astype(F32)
    there = r1[...].astype(F32) + r3[...].astype(F32)
    grad_conv[:, : C // 2] = jnp.where(core == 0, here, there)
    grad_conv[:, C // 2 :] = jnp.where(core == 0, there, here)


def last_qkv_kernel(where, r0, r1, r2, r3, grad_qkv, by_head):
    for mask, ref in enumerate((r0, r1, r2, r3)):
        by_head[where[0] ^ mask] = ref[...].astype(F32)

    def place(index, rows):
        grad_qkv[:, index * 128 : (index + 1) * 128] = rows

    for h in range(HEADS):
        place(h, by_head[h, :, :HK])
        place(HEADS + h, by_head[h, :, HK : 2 * HK])
    value_units(
        lambda index, rows: place(2 * HEADS + index, rows),
        [[by_head[h, :, (2 + k) * HK : (3 + k) * HK] for k in range(2)] for h in range(HEADS)],
    )


def last_stage(kernel, where, parts, dims, scratch=()):
    return pl.pallas_call(
        kernel,
        in_specs=[SMEM] + [VMEM] * 4,
        out_specs=VMEM,
        out_shape=shape(dims, F32),
        scratch_shapes=list(scratch),
        compiler_params=params(),
        name="last_stage",
    )(where, *parts)


def attended_kernel(where, a0, a1, a2, a3, out, by_head):
    for mask, ref in enumerate((a0, a1, a2, a3)):
        by_head[where[0] ^ mask] = ref[...]

    def place(index, rows):
        out[:, index * 128 : (index + 1) * 128] = rows

    value_units(
        place, [[by_head[h, :, k * HK : (k + 1) * HK] for k in range(2)] for h in range(HEADS)]
    )


def attended_rows(where, parts):
    return pl.pallas_call(
        attended_kernel,
        in_specs=[SMEM] + [VMEM] * 4,
        out_specs=VMEM,
        out_shape=shape((PAIRS, C)),
        scratch_shapes=[pltpu.VMEM((HEADS, PAIRS, WIN), BF16)],
        compiler_params=params(),
        name="attended_rows",
    )(where, *parts)


def shards(embedded, conv_weight, qkv_weight, cotangent):
    own = embedded[0]
    seq = lax.axis_index("seq")
    batch = lax.axis_index("batch")
    core, chip = seq % 2, seq // 2
    where = jnp.stack([seq, core, batch // 16, (batch // 4) % 4, batch % 4]).astype(jnp.int32)

    edges = jnp.concatenate([own[:8], own[-8:]])
    edge_same, edge_other = swap_seq(edges, 2), swap_seq(edges, 3)
    side = swap_seq(own, 1)
    far = swap_seq(own, 2)
    zero = jnp.zeros((8, C), F32)
    first = lambda a, b: jnp.where(core == 0, a, b)[:8].astype(F32)
    last = lambda a, b: jnp.where(core == 0, b, a)[8:].astype(F32)
    side_edges = jnp.concatenate([side[:8], side[-8:]])
    own_low = jnp.where(chip == 1, last(edge_same, edge_other), zero)
    own_high = jnp.where(chip == 0, first(edge_same, edge_other), zero)
    far_low = jnp.where(chip == 0, last(edges, side_edges), zero)
    far_high = jnp.where(chip == 1, first(edges, side_edges), zero)

    grads = []
    for mask in range(4):
        head = seq ^ mask
        piece = lax.dynamic_slice(cotangent[0], (0, ((3 * head) // 2) * HK), (PAIRS, WIN))
        grads.append(swap_seq(piece, mask) if mask else piece)

    first_column = ((3 * seq) // 2 + 2 * HEADS) * HK
    weight_own = jnp.concatenate(
        [
            lax.dynamic_slice(qkv_weight, (0, start), (2 * C, width))
            for start, width in ((seq * HK, HK), ((HEADS + seq) * HK, HK), (first_column, WIN))
        ],
        axis=1,
    )
    half = C // 2
    weight_rows = jnp.concatenate(
        [lax.dynamic_slice(qkv_weight, (p * C + core * half, 0), (half, 1792)) for p in range(2)]
    )

    joined_a, proj_a, columns = conv_chip(
        True, where, own, side, own_low, own_high, conv_weight, weight_own
    )
    far, weight_rows, proj_a = lax.optimization_barrier((far, weight_rows, proj_a))
    far_side = swap_seq(far, 1)
    joined_b, proj_b = conv_chip(
        False, where, far, far_side, far_low, far_high, conv_weight, weight_own
    )

    grad_a, grad_b, att_mine, att_side, att_b = attention(where, proj_a, proj_b, grads)

    far_grad = swap_seq(grad_b, 2)
    side_grad = swap_seq(grad_a, 1)
    qkv_blocks = qkv_gradient(joined_a, joined_b, grad_a, grad_b)
    far_grad, _ = lax.optimization_barrier((far_grad, qkv_blocks))
    qkv_blocks = over_plane(qkv_blocks)
    far_side_grad = swap_seq(far_grad, 1)
    conv_blocks = over_plane(
        conv_gradient(where, (grad_a, side_grad, far_grad, far_side_grad), weight_rows, columns)
    )

    att_b, _ = lax.optimization_barrier((att_b, far_grad))
    att_far = swap_seq(att_b, 2)
    attended = attended_rows(
        where, (att_mine, swap_seq(att_side, 1), att_far[0], swap_seq(att_far[1], 1))
    )

    def finish(blocks):
        pieces = sum_stage(where, blocks)
        parts = [pieces[0]] + [shift_batch(pieces[d], 0, d) for d in (1, 2, 3)]
        summed = sum(part.astype(F32) for part in parts).astype(BF16)
        return [summed] + [swap_seq(summed, mask) for mask in (1, 2, 3)]

    grad_qkv = last_stage(
        last_qkv_kernel,
        where,
        finish(qkv_blocks),
        (QR, 1792),
        [pltpu.VMEM((HEADS, QR, HD), F32)],
    )
    conv_blocks, grad_qkv, attended = lax.optimization_barrier((conv_blocks, grad_qkv, attended))
    grad_conv = last_stage(last_conv_kernel, where, finish(conv_blocks), (CR, C))
    return attended.reshape(1, PAIRS, HEADS * HV), grad_conv, grad_qkv


def solution(mesh):
    return jax.shard_map(
        shards,
        mesh=mesh,
        in_specs=(P("batch", "seq", None), P(), P(), P("batch", "seq", None)),
        out_specs=(P("batch", "seq", None), P("batch", None), P("batch", None)),
        check_vma=False,
    )
```

```python
import functools
import math

import jax
import jax.numpy as jnp
from jax import lax
from jax.experimental import pallas as pl
from jax.experimental.pallas import tpu as pltpu
from jax.sharding import PartitionSpec as P

HEADS = 4
HK = 128
HV = 192
WIN = 256
HD = 2 * HK + WIN
STEP = 4
C = 768
BINS = 512
PAIRS = 256
CHIP = 512
PAD = 8
CR = 36
QR = 24
QOFF = 112
JR = QOFF + 4 * QR
F32 = jnp.float32
BF16 = jnp.bfloat16

epsilon = 1e-06
temper = 1.0 / math.sqrt(HK)

VMEM = pl.BlockSpec(memory_space=pltpu.VMEM)
SMEM = pl.BlockSpec(memory_space=pltpu.SMEM)
HBM = pl.BlockSpec(memory_space=pltpu.HBM)


def params(mib):
    return pltpu.CompilerParams(vmem_limit_bytes=mib << 20)


def shape(dims, dtype=BF16):
    return jax.ShapeDtypeStruct(dims, dtype)


def cost(flops, nbytes):
    return pl.CostEstimate(flops=flops, bytes_accessed=nbytes, transcendentals=0)


def in_hbm(array):
    return pltpu.with_memory_space_constraint(array, pltpu.HBM)


def dot(a, b, ca=1, cb=0):
    return lax.dot_general(a, b, (((ca,), (cb,)), ((), ())), preferred_element_type=F32)


def swap_seq(block, mask):
    return lax.ppermute(block, "seq", [(i, i ^ mask) for i in range(4)])


def shift_batch(block, axis, distance):
    pairs = []
    for b in range(64):
        place = [b // 16, (b // 4) % 4, b % 4]
        place[axis] = (place[axis] + distance) % 4
        pairs.append((b, place[0] * 16 + place[1] * 4 + place[2]))
    return lax.ppermute(block, "batch", pairs)


def over_plane(blocks):
    groups = [[zh * 16 + place for place in range(16)] for zh in range(4)]
    return lax.all_to_all(
        blocks, "batch", split_axis=0, concat_axis=0, axis_index_groups=groups, tiled=True
    )


def sent(blocks, axis):
    return [blocks[0]] + [shift_batch(blocks[d], axis, d) for d in (1, 2, 3)]


def conv_kernel(keep, where, first, second, low, high, taps_hbm, weight_hbm, joined, proj, *refs):
    columns_hbm = refs[0] if keep else None
    act, stacked, bins, taps, weight, columns, sems, out_sem = refs[-8:]
    seq, core = where[0], where[1]
    loads = [pltpu.make_async_copy(taps_hbm, taps, sems.at[0])]
    for k, column in enumerate(
        (seq, HEADS + seq, 2 * HEADS + (3 * seq) // 2, 2 * HEADS + (3 * seq) // 2 + 1)
    ):
        source = weight_hbm.at[:, pl.ds(pl.multiple_of(column * HK, HK), HK)]
        loads.append(
            pltpu.make_async_copy(source, weight.at[:, k * HK : (k + 1) * HK], sems.at[1 + k])
        )
    for load in loads:
        load.start()
    for j in range(6):
        span = slice(j * 128, (j + 1) * 128)
        bins[j, 0:8, :] = low[:, span]
        here = pl.multiple_of(8 + core * BINS, 8)
        bins[j, pl.ds(here, BINS), :] = first[:, span].astype(F32)
        here = pl.multiple_of(8 + (1 - core) * BINS, 8)
        bins[j, pl.ds(here, BINS), :] = second[:, span].astype(F32)
        bins[j, 8 + 2 * BINS :, :] = high[:, span]

    def stream(parity, start, count):
        place = 8 + 2 * start + parity
        return jnp.concatenate(
            [bins[j, pl.ds(place, count, stride=2), :] for j in range(6)], axis=1
        )

    for parity in range(2):
        for start, count in ((-4, 4), (0, CHIP), (CHIP, 4)):
            act[PAD + start : PAD + start + count, :] = jax.nn.gelu(
                stream(parity, start, count), approximate=True
            )
        if keep and parity:
            pltpu.make_async_copy(columns, columns_hbm.at[0], out_sem).wait()
        for tap in range(3):
            start = PAD + (tap - 1) * (STEP // 2)
            rows = act[start : start + CHIP, :].astype(BF16)
            stacked[parity, :, tap * C : (tap + 1) * C] = rows
            if keep:
                columns[tap * C : (tap + 1) * C, :] = rows.T
        if keep:
            pltpu.make_async_copy(columns, columns_hbm.at[parity], out_sem).start()
        if parity == 0:
            loads[0].wait()
        out = stream(parity, 0, CHIP) + dot(stacked[parity], taps[...])
        joined[:, parity * C : (parity + 1) * C] = out.astype(BF16)
    for load in loads[1:]:
        load.wait()
    proj[...] = dot(joined[...], weight[...])
    if keep:
        pltpu.make_async_copy(columns, columns_hbm.at[1], out_sem).wait()


def conv_chip(keep, where, first, second, low, high, taps, weight):
    return pl.pallas_call(
        functools.partial(conv_kernel, keep),
        in_specs=[SMEM] + [VMEM] * 4 + [HBM] * 2,
        out_specs=[VMEM] * 2 + ([HBM] if keep else []),
        out_shape=[shape((CHIP, 2 * C)), shape((CHIP, HD), F32)]
        + ([pltpu.HBM((2, 3 * C, CHIP), BF16)] if keep else []),
        scratch_shapes=[
            pltpu.VMEM((CHIP + 2 * PAD, C), F32),
            pltpu.VMEM((2, CHIP, 3 * C), BF16),
            pltpu.VMEM((6, 2 * BINS + 16, 128), F32),
            pltpu.VMEM((3 * C, C), BF16),
            pltpu.VMEM((2 * C, HD), BF16),
            pltpu.VMEM((3 * C, CHIP) if keep else (8, 128), BF16),
            pltpu.SemaphoreType.DMA((5,)),
            pltpu.SemaphoreType.DMA,
        ],
        compiler_params=params(22),
        cost_estimate=cost(int(2 * 2 * 1024 * 3 * C * C) + 2 * CHIP * 2 * C * HD, 12 << 20)
        if keep
        else cost(1, 1),
        name="conv_own" if keep else "conv_far",
    )(where, first, second, low, high, in_hbm(taps), in_hbm(weight))


def unit(raw):
    return lax.rsqrt(jnp.mean(raw * raw, axis=-1, keepdims=True) + epsilon)


def unit_back(raw, grad_normed):
    factor = unit(raw)
    grad_f = grad_normed.astype(F32)
    inner = jnp.mean(grad_f * raw, axis=-1, keepdims=True)
    return (factor * grad_f - raw * factor * factor * factor * inner).astype(BF16)


def attention_kernel(
    where, proj_a, proj_b, g0, g1, g2, g3, grad_a, grad_b, att_mine, side_hbm, att_b_hbm,
    query, key, value, grad, key_sum, value_sum, att_side, att_b, sems,
):
    core = where[1]
    lane = lax.broadcasted_iota(jnp.int32, (CHIP, WIN), 1)
    valid = (lane >= 64 * core) & (lane < 64 * core + HV)
    for part, proj in enumerate((proj_a, proj_b)):
        rows = slice(part * CHIP, (part + 1) * CHIP)
        raw = proj[:, :HK]
        query[rows, :] = (raw * unit(raw)).astype(BF16)
        raw = proj[:, HK : 2 * HK]
        key[rows, :] = (raw * unit(raw)).astype(BF16)
        value[rows, :] = jnp.where(valid, proj[:, 2 * HK :], 0.0).astype(BF16)
    for part, pair in enumerate(((g0, g1), (g2, g3))):
        for side in range(2):
            place = pl.multiple_of(part * CHIP + (core ^ side) * PAIRS, PAIRS)
            grad[pl.ds(place, PAIRS), :] = pair[side][...]
    keys, values = key[...], value[...]
    for tile in range(4):
        rows = slice(tile * PAIRS, (tile + 1) * PAIRS)
        local = slice((tile % 2) * PAIRS, (tile % 2 + 1) * PAIRS)
        queries, grads = query[rows, :], grad[rows, :]
        expo = jnp.exp(dot(queries, keys, 1, 1) * temper)
        probs = expo * (1.0 / jnp.sum(expo, axis=-1, keepdims=True))
        probs_b = probs.astype(BF16)
        attended = dot(probs_b, values).astype(BF16)
        if tile < 2:

            @pl.when(core == tile)
            def _():
                att_mine[...] = attended

            @pl.when(core != tile)
            def _():
                att_side[...] = attended
        else:
            att_b[core ^ (tile - 2)] = attended
        grad_value = dot(probs_b, grads, 0, 0)
        grad_probs = dot(grads, values, 1, 1)
        inner = jnp.sum(probs * grad_probs, axis=-1, keepdims=True)
        grad_scores = (probs * (grad_probs - inner) * temper).astype(BF16)
        grad_query = dot(grad_scores, keys).astype(BF16)
        grad_key = dot(grad_scores, queries, 0, 0)
        if tile:
            value_sum[...] += grad_value
            key_sum[...] += grad_key
        else:
            value_sum[...] = grad_value
            key_sum[...] = grad_key
        proj, out = (proj_a, grad_a) if tile < 2 else (proj_b, grad_b)
        out[local, :HK] = unit_back(proj[local, :HK], grad_query)
    stores = [
        pltpu.make_async_copy(att_side, side_hbm, sems.at[0]),
        pltpu.make_async_copy(att_b, att_b_hbm, sems.at[1]),
    ]
    for store in stores:
        store.start()
    for part, (proj, out) in enumerate(((proj_a, grad_a), (proj_b, grad_b))):
        rows = slice(part * CHIP, (part + 1) * CHIP)
        out[:, HK : 2 * HK] = unit_back(proj[:, HK : 2 * HK], key_sum[rows, :].astype(BF16))
        out[:, 2 * HK :] = jnp.where(valid, value_sum[rows, :], 0.0).astype(BF16)
    for store in stores:
        store.wait()


def attention(where, proj_a, proj_b, grads):
    return pl.pallas_call(
        attention_kernel,
        in_specs=[SMEM] + [VMEM] * 6,
        out_specs=[VMEM] * 3 + [HBM] * 2,
        out_shape=[
            shape((CHIP, HD)),
            shape((CHIP, HD)),
            shape((PAIRS, WIN)),
            pltpu.HBM((PAIRS, WIN), BF16),
            pltpu.HBM((2, PAIRS, WIN), BF16),
        ],
        scratch_shapes=[
            pltpu.VMEM((2 * CHIP, HK), BF16),
            pltpu.VMEM((2 * CHIP, HK), BF16),
            pltpu.VMEM((2 * CHIP, WIN), BF16),
            pltpu.VMEM((2 * CHIP, WIN), BF16),
            pltpu.VMEM((2 * CHIP, HK), F32),
            pltpu.VMEM((2 * CHIP, WIN), F32),
            pltpu.VMEM((PAIRS, WIN), BF16),
            pltpu.VMEM((2, PAIRS, WIN), BF16),
            pltpu.SemaphoreType.DMA((2,)),
        ],
        compiler_params=params(18),
        cost_estimate=cost(6 * 2 * 1024 * 1024 * 192, 6 << 20),
        name="attention",
    )(where, proj_a, proj_b, *grads)


def qkv_kernel(joined_a, joined_b, grad_a, grad_b, out):
    for zh in range(4):
        columns = slice(zh * 16 * QR, (zh + 1) * 16 * QR)
        table = dot(joined_a[:, columns], grad_a[...], 0, 0) + dot(
            joined_b[:, columns], grad_b[...], 0, 0
        )
        for place in range(16):
            out[place, zh * QR : (zh + 1) * QR, :] = table[
                place * QR : (place + 1) * QR, :
            ].astype(BF16)


def qkv_gradient(joined_a, joined_b, grad_a, grad_b):
    return pl.pallas_call(
        qkv_kernel,
        in_specs=[VMEM] * 4,
        out_specs=VMEM,
        out_shape=shape((16, 4 * QR, HD)),
        compiler_params=params(14),
        cost_estimate=cost(2 * 1536 * 1024 * HD, 6 << 20),
        name="qkv_gradient",
    )(joined_a, joined_b, grad_a, grad_b)


def value_units(place, heads):
    place(0, heads[0][0])
    place(1, heads[0][1] + heads[1][0])
    place(2, heads[1][1])
    place(3, heads[2][0])
    place(4, heads[2][1] + heads[3][0])
    place(5, heads[3][1])


def conv_gradient_kernel(where, g0, g1, g2, g3, weight_hbm, columns_hbm, *refs):
    out_x, out_y = refs[:4], refs[4:8]
    by_head, natural, weight, columns, table, pieces, sems = refs[8:]
    seq, core, x, y = where[0], where[1], where[3], where[4]
    half = C // 2
    loads = []
    for p in range(2):
        source = weight_hbm.at[pl.ds(pl.multiple_of(p * C + core * half, half), half), :]
        loads.append(
            pltpu.make_async_copy(source, weight.at[p * half : (p + 1) * half, :], sems.at[p])
        )
    for p in range(2):
        loads.append(pltpu.make_async_copy(columns_hbm.at[p], columns.at[p], sems.at[2 + p]))
    for load in loads:
        load.start()
    for mask, ref in enumerate((g0, g1, g2, g3)):
        by_head[seq ^ mask] = ref[...]
    for h in range(HEADS):
        natural[:, h * HK : (h + 1) * HK] = by_head[h, :, :HK]
        natural[:, (HEADS + h) * HK : (HEADS + h + 1) * HK] = by_head[h, :, HK : 2 * HK]

    def place(index, rows):
        natural[:, (2 * HEADS + index) * HK : (2 * HEADS + index + 1) * HK] = rows

    value_units(
        place, [[by_head[h, :, (2 + k) * HK : (3 + k) * HK] for k in range(2)] for h in range(HEADS)]
    )
    loads[0].wait()
    loads[1].wait()
    hidden = dot(natural[...], weight[...], 1, 1).astype(BF16)
    loads[2].wait()
    loads[3].wait()
    block = 4 * CR
    for zh in range(4):
        rows = slice(zh * 4 * block, (zh + 1) * 4 * block)
        table[...] = dot(columns[0, rows, :], hidden[:, :half]) + dot(
            columns[1, rows, :], hidden[:, half:]
        )
        if zh < 2:
            for d in range(4):
                begin = pl.multiple_of(((x + d) % 4) * block, 8)
                out_x[d][zh] = table[pl.ds(begin, block), :].astype(BF16)
        else:
            for xx in range(4):
                chunk = table[xx * block : (xx + 1) * block, :]
                for yy in range(4):
                    pieces[(yy - y + 4) % 4, zh - 2, xx * CR : (xx + 1) * CR, :] = chunk[
                        yy * CR : (yy + 1) * CR, :
                    ]
    for d in range(4):
        out_y[d][...] = pieces[d].astype(BF16)


def conv_gradient(where, grads, weight, columns):
    return pl.pallas_call(
        conv_gradient_kernel,
        in_specs=[SMEM] + [VMEM] * 4 + [HBM] * 2,
        out_specs=[VMEM] * 8,
        out_shape=[shape((2, 4 * CR, C // 2))] * 8,
        scratch_shapes=[
            pltpu.VMEM((HEADS, CHIP, HD), BF16),
            pltpu.VMEM((CHIP, 1792), BF16),
            pltpu.VMEM((C, 1792), BF16),
            pltpu.VMEM((2, 3 * C, CHIP), BF16),
            pltpu.VMEM((16 * CR, C // 2), F32),
            pltpu.VMEM((4, 2, 4 * CR, C // 2), F32),
            pltpu.SemaphoreType.DMA((4,)),
        ],
        compiler_params=params(20),
        cost_estimate=cost(int(1 * (2 * CHIP * 1792 * C + 2 * 1024 * 3 * C * C // 2)), 1 << 20),
        name="conv_gradient",
    )(where, *grads, in_hbm(weight), in_hbm(columns))


def total(refs):
    out = refs[0][...].astype(F32)
    for ref in refs[1:]:
        out = out + ref[...].astype(F32)
    return out


def second_kernel(where, *refs):
    outs, pieces = refs[8:16], refs[16]
    for half, me in enumerate((where[4], where[3])):
        summed = total(refs[4 * half : 4 * half + 4])
        for k in range(4):
            pieces[(k - me + 4) % 4] = summed[:, k * CR : (k + 1) * CR, :]
        for d in range(4):
            outs[4 * half + d][...] = pieces[d].astype(BF16)


def second_stage(where, blocks):
    dims = (2, CR, C // 2)
    return pl.pallas_call(
        second_kernel,
        in_specs=[SMEM] + [VMEM] * 8,
        out_specs=[VMEM] * 8,
        out_shape=[shape(dims)] * 8,
        scratch_shapes=[pltpu.VMEM((4, *dims), F32)],
        compiler_params=params(10),
        name="second_stage",
    )(where, *blocks)


def sum_kernel(blocks, out):
    rows = blocks[0].astype(F32)
    for place in range(1, 16):
        rows = rows + blocks[place].astype(F32)
    out[...] = rows


def sum_stage(blocks):
    return pl.pallas_call(
        sum_kernel,
        in_specs=[VMEM],
        out_specs=VMEM,
        out_shape=shape(blocks.shape[1:], F32),
        compiler_params=params(8),
        name="sum_stage",
    )(blocks)


def joint_kernel(where, qkv, *refs):
    conv, outs, pieces = refs[:8], refs[8:12], refs[12]
    halves = [total(conv[:4]), total(conv[4:])]
    for zh in range(4):
        for j in range(3):
            pieces[zh, j * CR : (j + 1) * CR, :] = halves[zh // 2][
                zh % 2, :, j * 128 : (j + 1) * 128
            ]
        pieces[zh, 3 * CR : QOFF, :] = jnp.zeros((QOFF - 3 * CR, 128), F32)
        for j in range(4):
            pieces[zh, QOFF + j * QR : QOFF + (j + 1) * QR, :] = qkv[
                zh * QR : (zh + 1) * QR, j * 128 : (j + 1) * 128
            ]
    for d in range(4):
        outs[d][...] = pieces[(where[2] + d) % 4].astype(BF16)


def joint_stage(where, qkv, conv):
    return pl.pallas_call(
        joint_kernel,
        in_specs=[SMEM] + [VMEM] * 9,
        out_specs=[VMEM] * 4,
        out_shape=[shape((JR, 128))] * 4,
        scratch_shapes=[pltpu.VMEM((4, JR, 128), F32)],
        compiler_params=params(6),
        name="joint_stage",
    )(where, qkv, *conv)


def last_kernel(where, r0, r1, r2, r3, grad_conv, grad_qkv, by_head):
    seq, core = where[0], where[1]
    parts = [ref[...].astype(F32) for ref in (r0, r1, r2, r3)]
    here = parts[0] + parts[2]
    there = parts[1] + parts[3]
    low = jnp.where(core == 0, here, there)
    high = jnp.where(core == 0, there, here)
    for j in range(3):
        span = slice(j * CR, (j + 1) * CR)
        grad_conv[:, j * 128 : (j + 1) * 128] = low[span, :]
        grad_conv[:, (3 + j) * 128 : (4 + j) * 128] = high[span, :]
    for mask in range(4):
        by_head[seq ^ mask] = parts[mask][QOFF:, :]

    def place(index, rows):
        grad_qkv[:, index * 128 : (index + 1) * 128] = rows

    for h in range(HEADS):
        place(h, by_head[h, :QR, :])
        place(HEADS + h, by_head[h, QR : 2 * QR, :])
    value_units(
        lambda index, rows: place(2 * HEADS + index, rows),
        [[by_head[h, (2 + k) * QR : (3 + k) * QR, :] for k in range(2)] for h in range(HEADS)],
    )


def last_stage(where, parts):
    return pl.pallas_call(
        last_kernel,
        in_specs=[SMEM] + [VMEM] * 4,
        out_specs=[VMEM] * 2,
        out_shape=[shape((CR, C), F32), shape((QR, 1792), F32)],
        scratch_shapes=[pltpu.VMEM((HEADS, 4 * QR, 128), F32)],
        compiler_params=params(4),
        name="last_stage",
    )(where, *parts)


def attended_kernel(where, a0, a1, a2, a3, out, by_head):
    for mask, ref in enumerate((a0, a1, a2, a3)):
        by_head[where[0] ^ mask] = ref[...]

    def place(index, rows):
        out[:, index * 128 : (index + 1) * 128] = rows

    value_units(
        place, [[by_head[h, :, k * HK : (k + 1) * HK] for k in range(2)] for h in range(HEADS)]
    )


def attended_rows(where, parts):
    return pl.pallas_call(
        attended_kernel,
        in_specs=[SMEM] + [VMEM] * 4,
        out_specs=VMEM,
        out_shape=shape((PAIRS, C)),
        scratch_shapes=[pltpu.VMEM((HEADS, PAIRS, WIN), BF16)],
        compiler_params=params(4),
        name="attended_rows",
    )(where, *parts)


def shards(embedded, conv_weight, qkv_weight, cotangent):
    own = embedded[0]
    seq = lax.axis_index("seq")
    batch = lax.axis_index("batch")
    core, chip = seq % 2, seq // 2
    where = jnp.stack([seq, core, batch // 16, (batch // 4) % 4, batch % 4]).astype(jnp.int32)

    edges = jnp.concatenate([own[:8], own[-8:]])
    own, edges = lax.optimization_barrier((own, edges))
    edge_same, edge_other = swap_seq(edges, 2), swap_seq(edges, 3)
    side = swap_seq(own, 1)
    far = swap_seq(own, 2)
    zero = jnp.zeros((8, C), F32)
    first = lambda a, b: jnp.where(core == 0, a, b)[:8].astype(F32)
    last = lambda a, b: jnp.where(core == 0, b, a)[8:].astype(F32)
    side_edges = jnp.concatenate([side[:8], side[-8:]])
    own_low = jnp.where(chip == 1, last(edge_same, edge_other), zero)
    own_high = jnp.where(chip == 0, first(edge_same, edge_other), zero)
    far_low = jnp.where(chip == 0, last(edges, side_edges), zero)
    far_high = jnp.where(chip == 1, first(edges, side_edges), zero)

    grads = []
    for mask in range(4):
        head = seq ^ mask
        piece = lax.dynamic_slice(cotangent[0], (0, ((3 * head) // 2) * HK), (PAIRS, WIN))
        grads.append(swap_seq(piece, mask) if mask else piece)

    joined_a, proj_a, columns = conv_chip(
        True, where, own, side, own_low, own_high, conv_weight, qkv_weight
    )
    far, proj_a = lax.optimization_barrier((far, proj_a))
    far_side = swap_seq(far, 1)
    joined_b, proj_b = conv_chip(
        False, where, far, far_side, far_low, far_high, conv_weight, qkv_weight
    )

    grad_a, grad_b, att_mine, att_side, att_b = attention(where, proj_a, proj_b, grads)

    far_grad = swap_seq(grad_b, 2)
    side_grad = swap_seq(grad_a, 1)
    qkv_blocks = qkv_gradient(joined_a, joined_b, grad_a, grad_b)
    far_grad, _ = lax.optimization_barrier((far_grad, qkv_blocks))
    qkv_blocks = over_plane(qkv_blocks)
    far_side_grad = swap_seq(far_grad, 1)
    conv_blocks = conv_gradient(
        where, (grad_a, side_grad, far_grad, far_side_grad), qkv_weight, columns
    )

    att_b, _ = lax.optimization_barrier((att_b, far_grad))
    att_far = swap_seq(att_b, 2)
    attended = attended_rows(
        where, (att_mine, swap_seq(att_side, 1), att_far[0], swap_seq(att_far[1], 1))
    )

    conv_blocks = sent(conv_blocks[:4], 1) + sent(conv_blocks[4:], 2)
    qkv_sum = sum_stage(qkv_blocks)
    conv_blocks, qkv_sum = lax.optimization_barrier((conv_blocks, qkv_sum))
    conv_blocks = second_stage(where, conv_blocks)
    conv_blocks = sent(conv_blocks[:4], 2) + sent(conv_blocks[4:], 1)
    conv_blocks, attended = lax.optimization_barrier((conv_blocks, attended))
    parts = sent(joint_stage(where, qkv_sum, conv_blocks), 0)
    summed = sum(part.astype(F32) for part in parts).astype(BF16)
    grad_conv, grad_qkv = last_stage(
        where, [summed] + [swap_seq(summed, mask) for mask in (1, 2, 3)]
    )
    return attended.reshape(1, PAIRS, HEADS * HV), grad_conv, grad_qkv


def solution(mesh):
    return jax.shard_map(
        shards,
        mesh=mesh,
        in_specs=(P("batch", "seq", None), P(), P(), P("batch", "seq", None)),
        out_specs=(P("batch", "seq", None), P("batch", None), P("batch", None)),
        check_vma=False,
    )
```

```python
import functools
import math

import jax
import jax.numpy as jnp
from jax import lax
from jax.experimental import pallas as pl
from jax.experimental.pallas import tpu as pltpu
from jax.sharding import PartitionSpec as P

HEADS = 4
HK = 128
HV = 192
WIN = 256
HD = 2 * HK + WIN
STEP = 4
C = 768
BINS = 512
PAIRS = 256
CHIP = 512
PAD = 8
CR = 36
QR = 24
F32 = jnp.float32
BF16 = jnp.bfloat16

epsilon = 1e-06
temper = 1.0 / math.sqrt(HK)

VMEM = pl.BlockSpec(memory_space=pltpu.VMEM)
SMEM = pl.BlockSpec(memory_space=pltpu.SMEM)
HBM = pl.BlockSpec(memory_space=pltpu.HBM)


def params(mib):
    return pltpu.CompilerParams(vmem_limit_bytes=mib << 20)


def shape(dims, dtype=BF16):
    return jax.ShapeDtypeStruct(dims, dtype)


def cost(flops, nbytes):
    return pl.CostEstimate(flops=flops, bytes_accessed=nbytes, transcendentals=0)


def in_hbm(array):
    return pltpu.with_memory_space_constraint(array, pltpu.HBM)


def dot(a, b, ca=1, cb=0):
    return lax.dot_general(a, b, (((ca,), (cb,)), ((), ())), preferred_element_type=F32)


def swap_seq(block, mask):
    return lax.ppermute(block, "seq", [(i, i ^ mask) for i in range(4)])


def shift_batch(block, axis, distance):
    pairs = []
    for b in range(64):
        place = [b // 16, (b // 4) % 4, b % 4]
        place[axis] = (place[axis] + distance) % 4
        pairs.append((b, place[0] * 16 + place[1] * 4 + place[2]))
    return lax.ppermute(block, "batch", pairs)


def over_plane(blocks):
    groups = [[zh * 16 + place for place in range(16)] for zh in range(4)]
    return lax.all_to_all(
        blocks, "batch", split_axis=0, concat_axis=0, axis_index_groups=groups, tiled=True
    )


def over_column(blocks):
    groups = [
        [(zh * 16 + place) * 4 + seq for zh in range(4) for seq in range(4)] for place in range(16)
    ]
    return lax.all_to_all(
        blocks, ("batch", "seq"), split_axis=0, concat_axis=0, axis_index_groups=groups, tiled=True
    )


def conv_kernel(keep, where, first, second, low, high, taps_hbm, weight_hbm, joined, proj, *refs):
    columns_hbm = refs[0] if keep else None
    act, stacked, bins, taps, weight, columns, sems, out_sem = refs[-8:]
    seq, core = where[0], where[1]
    loads = [pltpu.make_async_copy(taps_hbm, taps, sems.at[0])]
    for k, column in enumerate(
        (seq, HEADS + seq, 2 * HEADS + (3 * seq) // 2, 2 * HEADS + (3 * seq) // 2 + 1)
    ):
        source = weight_hbm.at[:, pl.ds(pl.multiple_of(column * HK, HK), HK)]
        loads.append(
            pltpu.make_async_copy(source, weight.at[:, k * HK : (k + 1) * HK], sems.at[1 + k])
        )
    for load in loads:
        load.start()
    for j in range(6):
        span = slice(j * 128, (j + 1) * 128)
        bins[j, 0:8, :] = low[:, span]
        here = pl.multiple_of(8 + core * BINS, 8)
        bins[j, pl.ds(here, BINS), :] = first[:, span].astype(F32)
        here = pl.multiple_of(8 + (1 - core) * BINS, 8)
        bins[j, pl.ds(here, BINS), :] = second[:, span].astype(F32)
        bins[j, 8 + 2 * BINS :, :] = high[:, span]

    def stream(parity, start, count):
        place = 8 + 2 * start + parity
        return jnp.concatenate(
            [bins[j, pl.ds(place, count, stride=2), :] for j in range(6)], axis=1
        )

    for parity in range(2):
        for start, count in ((-4, 4), (0, CHIP), (CHIP, 4)):
            act[PAD + start : PAD + start + count, :] = jax.nn.gelu(
                stream(parity, start, count), approximate=True
            )
        if keep and parity:
            pltpu.make_async_copy(columns, columns_hbm.at[0], out_sem).wait()
        for tap in range(3):
            start = PAD + (tap - 1) * (STEP // 2)
            rows = act[start : start + CHIP, :].astype(BF16)
            stacked[parity, :, tap * C : (tap + 1) * C] = rows
            if keep:
                columns[tap * C : (tap + 1) * C, :] = rows.T
        if keep:
            pltpu.make_async_copy(columns, columns_hbm.at[parity], out_sem).start()
        if parity == 0:
            loads[0].wait()
        out = stream(parity, 0, CHIP) + dot(stacked[parity], taps[...])
        joined[:, parity * C : (parity + 1) * C] = out.astype(BF16)
    for load in loads[1:]:
        load.wait()
    proj[...] = dot(joined[...], weight[...])
    if keep:
        pltpu.make_async_copy(columns, columns_hbm.at[1], out_sem).wait()


def conv_chip(keep, where, first, second, low, high, taps, weight):
    return pl.pallas_call(
        functools.partial(conv_kernel, keep),
        in_specs=[SMEM] + [VMEM] * 4 + [HBM] * 2,
        out_specs=[VMEM] * 2 + ([HBM] if keep else []),
        out_shape=[shape((CHIP, 2 * C)), shape((CHIP, HD), F32)]
        + ([pltpu.HBM((2, 3 * C, CHIP), BF16)] if keep else []),
        scratch_shapes=[
            pltpu.VMEM((CHIP + 2 * PAD, C), F32),
            pltpu.VMEM((2, CHIP, 3 * C), BF16),
            pltpu.VMEM((6, 2 * BINS + 16, 128), F32),
            pltpu.VMEM((3 * C, C), BF16),
            pltpu.VMEM((2 * C, HD), BF16),
            pltpu.VMEM((3 * C, CHIP) if keep else (8, 128), BF16),
            pltpu.SemaphoreType.DMA((5,)),
            pltpu.SemaphoreType.DMA,
        ],
        compiler_params=params(22),
        cost_estimate=cost(2 * 2 * 1024 * 3 * C * C + 2 * CHIP * 2 * C * HD, 12 << 20),
        name="conv_own",
    )(where, first, second, low, high, in_hbm(taps), in_hbm(weight))


def block_kernel(where, rows, low, high, taps_hbm, weight_hbm, joined, proj, *refs):
    act, stacked, bins, taps, weight, sems = refs
    seq = where[0]
    loads = [pltpu.make_async_copy(taps_hbm, taps, sems.at[0])]
    for k, column in enumerate(
        (seq, HEADS + seq, 2 * HEADS + (3 * seq) // 2, 2 * HEADS + (3 * seq) // 2 + 1)
    ):
        source = weight_hbm.at[:, pl.ds(pl.multiple_of(column * HK, HK), HK)]
        loads.append(
            pltpu.make_async_copy(source, weight.at[:, k * HK : (k + 1) * HK], sems.at[1 + k])
        )
    for load in loads:
        load.start()
    for j in range(6):
        span = slice(j * 128, (j + 1) * 128)
        bins[j, 0:8, :] = low[:, span]
        bins[j, 8 : 8 + BINS, :] = rows[:, span].astype(F32)
        bins[j, 8 + BINS :, :] = high[:, span]

    def stream(parity, part, start, count):
        place = 8 + 2 * start + parity
        return jnp.concatenate(
            [bins[j, pl.ds(place, count, stride=2), :] for j in (2 * part, 2 * part + 1)], axis=1
        )

    def fill(parity, part):
        span = slice(part * 256, (part + 1) * 256)
        for start, count in ((-4, 4), (0, PAIRS), (PAIRS, 4)):
            act[parity, PAD + start : PAD + start + count, span] = jax.nn.gelu(
                stream(parity, part, start, count), approximate=True
            )
        for tap in range(3):
            start = PAD + (tap - 1) * (STEP // 2)
            column = tap * C + part * 256
            stacked[parity, :, column : column + 256] = act[
                parity, start : start + PAIRS, span
            ].astype(BF16)

    def convolve(parity, part):
        span = slice(part * 256, (part + 1) * 256)
        out = stream(parity, part, 0, PAIRS) + dot(stacked[parity], taps[:, span])
        column = parity * C + part * 256
        joined[:, column : column + 256] = out.astype(BF16)

    for part in range(3):
        fill(0, part)
    loads[0].wait()
    for part in range(3):
        convolve(0, part)
        fill(1, part)
    for part in range(3):
        convolve(1, part)
    for load in loads[1:]:
        load.wait()
    proj[...] = dot(joined[...], weight[...])


def conv_block(where, rows, low, high, taps, weight):
    return pl.pallas_call(
        block_kernel,
        in_specs=[SMEM] + [VMEM] * 3 + [HBM] * 2,
        out_specs=[VMEM] * 2,
        out_shape=[shape((PAIRS, 2 * C)), shape((PAIRS, HD), F32)],
        scratch_shapes=[
            pltpu.VMEM((2, PAIRS + 2 * PAD, C), F32),
            pltpu.VMEM((2, PAIRS, 3 * C), BF16),
            pltpu.VMEM((6, BINS + 16, 128), F32),
            pltpu.VMEM((3 * C, C), BF16),
            pltpu.VMEM((2 * C, HD), BF16),
            pltpu.SemaphoreType.DMA((5,)),
        ],
        compiler_params=params(18),
        cost_estimate=cost(1, 1),
        name="conv_block",
    )(where, rows, low, high, in_hbm(taps), in_hbm(weight))


def unit(raw):
    return lax.rsqrt(jnp.mean(raw * raw, axis=-1, keepdims=True) + epsilon)


def unit_back(raw, grad_normed):
    factor = unit(raw)
    grad_f = grad_normed.astype(F32)
    inner = jnp.mean(grad_f * raw, axis=-1, keepdims=True)
    return (factor * grad_f - raw * factor * factor * factor * inner).astype(BF16)


def attention_kernel(
    where, proj_a, proj_c, proj_d, g0, g1, g2, g3, grad_a, grad_b, att_mine, side_hbm, att_b_hbm,
    query, key, value, grad, key_sum, value_sum, att_side, att_b, sems,
):
    core = where[1]
    lane = lax.broadcasted_iota(jnp.int32, (CHIP, WIN), 1)
    valid = (lane >= 64 * core) & (lane < 64 * core + HV)
    for start, proj in ((0, proj_a), (CHIP, proj_c), (CHIP + PAIRS, proj_d)):
        count = proj.shape[0]
        rows = slice(start, start + count)
        raw = proj[:, :HK]
        query[rows, :] = (raw * unit(raw)).astype(BF16)
        raw = proj[:, HK : 2 * HK]
        key[rows, :] = (raw * unit(raw)).astype(BF16)
        value[rows, :] = jnp.where(valid[:count], proj[:, 2 * HK :], 0.0).astype(BF16)
    for side, ref in enumerate((g0, g1)):
        grad[pl.ds(pl.multiple_of((core ^ side) * PAIRS, PAIRS), PAIRS), :] = ref[...]
    grad[CHIP : CHIP + PAIRS, :] = g2[...]
    grad[CHIP + PAIRS :, :] = g3[...]
    keys, values = key[...], value[...]
    for tile in range(4):
        rows = slice(tile * PAIRS, (tile + 1) * PAIRS)
        local = slice((tile % 2) * PAIRS, (tile % 2 + 1) * PAIRS)
        queries, grads = query[rows, :], grad[rows, :]
        expo = jnp.exp(dot(queries, keys, 1, 1) * temper)
        probs = expo * (1.0 / jnp.sum(expo, axis=-1, keepdims=True))
        probs_b = probs.astype(BF16)
        attended = dot(probs_b, values).astype(BF16)
        if tile < 2:

            @pl.when(core == tile)
            def _():
                att_mine[...] = attended

            @pl.when(core != tile)
            def _():
                att_side[...] = attended
        else:
            att_b[tile - 2] = attended
        grad_value = dot(probs_b, grads, 0, 0)
        grad_probs = dot(grads, values, 1, 1)
        inner = jnp.sum(probs * grad_probs, axis=-1, keepdims=True)
        grad_scores = (probs * (grad_probs - inner) * temper).astype(BF16)
        grad_query = dot(grad_scores, keys).astype(BF16)
        grad_key = dot(grad_scores, queries, 0, 0)
        if tile:
            value_sum[...] += grad_value
            key_sum[...] += grad_key
        else:
            value_sum[...] = grad_value
            key_sum[...] = grad_key
        if tile < 2:
            grad_a[local, :HK] = unit_back(proj_a[local, :HK], grad_query)
        else:
            proj = (proj_c, proj_d)[tile - 2]
            place = pl.multiple_of((core ^ (tile - 2)) * PAIRS, PAIRS)
            grad_b[pl.ds(place, PAIRS), :HK] = unit_back(proj[:, :HK], grad_query)
    stores = [
        pltpu.make_async_copy(att_side, side_hbm, sems.at[0]),
        pltpu.make_async_copy(att_b, att_b_hbm, sems.at[1]),
    ]
    for store in stores:
        store.start()
    rows = slice(0, CHIP)
    grad_a[:, HK : 2 * HK] = unit_back(proj_a[:, HK : 2 * HK], key_sum[rows, :].astype(BF16))
    grad_a[:, 2 * HK :] = jnp.where(valid, value_sum[rows, :], 0.0).astype(BF16)
    for side, proj in enumerate((proj_c, proj_d)):
        rows = slice(CHIP + side * PAIRS, CHIP + (side + 1) * PAIRS)
        place = pl.ds(pl.multiple_of((core ^ side) * PAIRS, PAIRS), PAIRS)
        grad_b[place, HK : 2 * HK] = unit_back(
            proj[:, HK : 2 * HK], key_sum[rows, :].astype(BF16)
        )
        grad_b[place, 2 * HK :] = jnp.where(valid[:PAIRS], value_sum[rows, :], 0.0).astype(BF16)
    for store in stores:
        store.wait()


def attention(where, proj_a, proj_c, proj_d, grads):
    return pl.pallas_call(
        attention_kernel,
        in_specs=[SMEM] + [VMEM] * 7,
        out_specs=[VMEM] * 3 + [HBM] * 2,
        out_shape=[
            shape((CHIP, HD)),
            shape((CHIP, HD)),
            shape((PAIRS, WIN)),
            pltpu.HBM((PAIRS, WIN), BF16),
            pltpu.HBM((2, PAIRS, WIN), BF16),
        ],
        scratch_shapes=[
            pltpu.VMEM((2 * CHIP, HK), BF16),
            pltpu.VMEM((2 * CHIP, HK), BF16),
            pltpu.VMEM((2 * CHIP, WIN), BF16),
            pltpu.VMEM((2 * CHIP, WIN), BF16),
            pltpu.VMEM((2 * CHIP, HK), F32),
            pltpu.VMEM((2 * CHIP, WIN), F32),
            pltpu.VMEM((PAIRS, WIN), BF16),
            pltpu.VMEM((2, PAIRS, WIN), BF16),
            pltpu.SemaphoreType.DMA((2,)),
        ],
        compiler_params=params(18),
        cost_estimate=cost(6 * 2 * 1024 * 1024 * 192, 6 << 20),
        name="attention",
    )(where, proj_a, proj_c, proj_d, *grads)


def qkv_kernel(where, joined_a, joined_c, joined_d, grad_a, grad_b, out_hbm, staged, sems):
    core = where[1]
    near = grad_b[pl.ds(pl.multiple_of(core * PAIRS, PAIRS), PAIRS), :]
    side = grad_b[pl.ds(pl.multiple_of((1 - core) * PAIRS, PAIRS), PAIRS), :]
    stores = []
    for zh in range(4):
        columns = slice(zh * 16 * QR, (zh + 1) * 16 * QR)
        table = (
            dot(joined_a[:, columns], grad_a[...], 0, 0)
            + dot(joined_c[:, columns], near, 0, 0)
            + dot(joined_d[:, columns], side, 0, 0)
        )
        span = slice(zh * QR, (zh + 1) * QR)
        for place in range(16):
            staged[place, span, :] = table[place * QR : (place + 1) * QR, :].astype(BF16)
        if zh % 2:
            span = slice((zh - 1) * QR, (zh + 1) * QR)
            stores.append(
                pltpu.make_async_copy(
                    staged.at[:, span, :], out_hbm.at[:, span, :], sems.at[zh // 2]
                )
            )
            stores[-1].start()
    for store in stores:
        store.wait()


def qkv_gradient(where, joined_a, joined_c, joined_d, grad_a, grad_b):
    return pl.pallas_call(
        qkv_kernel,
        in_specs=[SMEM] + [VMEM] * 5,
        out_specs=HBM,
        out_shape=pltpu.HBM((16, 4 * QR, HD), BF16),
        scratch_shapes=[
            pltpu.VMEM((16, 4 * QR, HD), BF16),
            pltpu.SemaphoreType.DMA((2,)),
        ],
        compiler_params=params(14),
        cost_estimate=cost(2 * 1536 * 1024 * HD, 6 << 20),
        name="qkv_gradient",
    )(where, joined_a, joined_c, joined_d, grad_a, grad_b)


def value_units(place, heads):
    place(0, heads[0][0])
    place(1, heads[0][1] + heads[1][0])
    place(2, heads[1][1])
    place(3, heads[2][0])
    place(4, heads[2][1] + heads[3][0])
    place(5, heads[3][1])


def conv_gradient_kernel(
    where, g0, g1, g2, g3, weight_hbm, columns_hbm, out_hbm,
    by_head, natural, weight, columns, staged, sems, out_sems,
):
    seq, core = where[0], where[1]
    half = C // 2
    loads = []
    for p in range(2):
        source = weight_hbm.at[pl.ds(pl.multiple_of(p * C + core * half, half), half), :]
        loads.append(
            pltpu.make_async_copy(source, weight.at[p * half : (p + 1) * half, :], sems.at[p])
        )
    for p in range(2):
        loads.append(pltpu.make_async_copy(columns_hbm.at[p], columns.at[p], sems.at[2 + p]))
    for load in loads:
        load.start()
    for mask, ref in enumerate((g0, g1, g2, g3)):
        by_head[seq ^ mask] = ref[...]
    for h in range(HEADS):
        natural[:, h * HK : (h + 1) * HK] = by_head[h, :, :HK]
        natural[:, (HEADS + h) * HK : (HEADS + h + 1) * HK] = by_head[h, :, HK : 2 * HK]

    def place(index, rows):
        natural[:, (2 * HEADS + index) * HK : (2 * HEADS + index + 1) * HK] = rows

    value_units(
        place, [[by_head[h, :, (2 + k) * HK : (3 + k) * HK] for k in range(2)] for h in range(HEADS)]
    )
    loads[0].wait()
    loads[1].wait()
    hidden = dot(natural[...], weight[...], 1, 1).astype(BF16)
    loads[2].wait()
    loads[3].wait()
    stores = []
    for zh in range(4):
        rows = slice(zh * 16 * CR, (zh + 1) * 16 * CR)
        table = dot(columns[0, rows, :], hidden[:, :half]) + dot(
            columns[1, rows, :], hidden[:, half:]
        )
        for block in range(16):
            staged[block, zh * CR : (zh + 1) * CR, :] = table[
                block * CR : (block + 1) * CR, :
            ].astype(BF16)
        if zh % 2:
            span = slice((zh - 1) * CR, (zh + 1) * CR)
            stores.append(
                pltpu.make_async_copy(
                    staged.at[:, span, :], out_hbm.at[:, span, :], out_sems.at[zh // 2]
                )
            )
            stores[-1].start()
    for store in stores:
        store.wait()


def conv_gradient(where, grads, weight, columns):
    return pl.pallas_call(
        conv_gradient_kernel,
        in_specs=[SMEM] + [VMEM] * 4 + [HBM] * 2,
        out_specs=HBM,
        out_shape=pltpu.HBM((16, 4 * CR, C // 2), BF16),
        scratch_shapes=[
            pltpu.VMEM((HEADS, CHIP, HD), BF16),
            pltpu.VMEM((CHIP, 1792), BF16),
            pltpu.VMEM((C, 1792), BF16),
            pltpu.VMEM((2, 3 * C, CHIP), BF16),
            pltpu.VMEM((16, 4 * CR, C // 2), BF16),
            pltpu.SemaphoreType.DMA((4,)),
            pltpu.SemaphoreType.DMA((2,)),
        ],
        compiler_params=params(26),
        cost_estimate=cost(2 * (2 * CHIP * 1792 * C + 2 * 1024 * 3 * C * C // 2), 10 << 20),
        name="conv_gradient",
    )(where, *grads, in_hbm(weight), in_hbm(columns))


def sum_kernel(where, blocks, *refs):
    outs, sums = refs[:4], refs[4]
    out = blocks[0].astype(F32)
    for place in range(1, 16):
        out = out + blocks[place].astype(F32)
    rows = sums.shape[1]
    for zh in range(4):
        sums[zh] = out[zh * rows : (zh + 1) * rows, :]
    for d in range(4):
        outs[d][...] = sums[(where[2] + d) % 4].astype(BF16)


def sum_stage(where, blocks):
    dims = (blocks.shape[1] // 4, blocks.shape[2])
    return pl.pallas_call(
        sum_kernel,
        in_specs=[SMEM, VMEM],
        out_specs=[VMEM] * 4,
        out_shape=[shape(dims)] * 4,
        scratch_shapes=[pltpu.VMEM((4, *dims), F32)],
        compiler_params=params(10),
        name="sum_stage",
    )(where, blocks)


def spread_kernel(blocks, out):
    rows = blocks[0].astype(F32)
    for place in range(1, 16):
        rows = rows + blocks[place].astype(F32)
    for zh in range(4):
        piece = rows[zh * CR : (zh + 1) * CR, :].astype(BF16)
        for s in range(4):
            out[4 * zh + s] = piece


def spread_stage(blocks):
    return pl.pallas_call(
        spread_kernel,
        in_specs=[VMEM],
        out_specs=VMEM,
        out_shape=shape((16, CR, C // 2)),
        compiler_params=params(10),
        name="spread_stage",
    )(blocks)


def last_conv_kernel(blocks, grad_conv):
    for core in range(2):
        rows = blocks[core].astype(F32) + blocks[core + 2].astype(F32)
        for zh in range(1, 4):
            rows = rows + blocks[4 * zh + core].astype(F32)
            rows = rows + blocks[4 * zh + core + 2].astype(F32)
        grad_conv[:, core * (C // 2) : (core + 1) * (C // 2)] = rows


def last_conv(blocks):
    return pl.pallas_call(
        last_conv_kernel,
        in_specs=[VMEM],
        out_specs=VMEM,
        out_shape=shape((CR, C), F32),
        compiler_params=params(6),
        name="last_conv",
    )(blocks)


def last_qkv_kernel(where, r0, r1, r2, r3, grad_qkv, by_head):
    for mask, ref in enumerate((r0, r1, r2, r3)):
        by_head[where[0] ^ mask] = ref[...].astype(F32)

    def place(index, rows):
        grad_qkv[:, index * 128 : (index + 1) * 128] = rows

    for h in range(HEADS):
        place(h, by_head[h, :, :HK])
        place(HEADS + h, by_head[h, :, HK : 2 * HK])
    value_units(
        lambda index, rows: place(2 * HEADS + index, rows),
        [[by_head[h, :, (2 + k) * HK : (3 + k) * HK] for k in range(2)] for h in range(HEADS)],
    )


def last_stage(kernel, where, parts, dims, scratch=()):
    return pl.pallas_call(
        kernel,
        in_specs=[SMEM] + [VMEM] * 4,
        out_specs=VMEM,
        out_shape=shape(dims, F32),
        scratch_shapes=list(scratch),
        compiler_params=params(4),
        name="last_stage",
    )(where, *parts)


def attended_kernel(where, a0, a1, a2, a3, out, by_head):
    for mask, ref in enumerate((a0, a1, a2, a3)):
        by_head[where[0] ^ mask] = ref[...]

    def place(index, rows):
        out[:, index * 128 : (index + 1) * 128] = rows

    value_units(
        place, [[by_head[h, :, k * HK : (k + 1) * HK] for k in range(2)] for h in range(HEADS)]
    )


def attended_rows(where, parts):
    return pl.pallas_call(
        attended_kernel,
        in_specs=[SMEM] + [VMEM] * 4,
        out_specs=VMEM,
        out_shape=shape((PAIRS, C)),
        scratch_shapes=[pltpu.VMEM((HEADS, PAIRS, WIN), BF16)],
        compiler_params=params(4),
        name="attended_rows",
    )(where, *parts)


def shards(embedded, conv_weight, qkv_weight, cotangent):
    own = embedded[0]
    seq = lax.axis_index("seq")
    batch = lax.axis_index("batch")
    core, chip = seq % 2, seq // 2
    where = jnp.stack([seq, core, batch // 16, (batch // 4) % 4, batch % 4]).astype(jnp.int32)

    edges = jnp.concatenate([own[:8], own[-8:]])
    own, edges = lax.optimization_barrier((own, edges))
    edge_same, edge_other = swap_seq(edges, 2), swap_seq(edges, 3)
    side = swap_seq(own, 1)
    far = swap_seq(own, 2)
    zero = jnp.zeros((8, C), F32)
    side_edges = jnp.concatenate([side[:8], side[-8:]])
    ordered = lambda a, b: [jnp.where(core == k, a, b).astype(F32) for k in range(2)]
    mine, theirs = ordered(edges, side_edges), ordered(edge_same, edge_other)
    own_low = jnp.where(chip == 1, theirs[1][8:], zero)
    own_high = jnp.where(chip == 0, theirs[0][:8], zero)
    low, high = theirs[0][8:], theirs[1][:8]
    outer_low = jnp.where(chip == 0, mine[1][8:], zero)
    outer_high = jnp.where(chip == 1, mine[0][:8], zero)
    far_halo = [
        (jnp.where(second, low, outer_low), jnp.where(second, outer_high, high))
        for second in (core == 1, core == 0)
    ]

    grads = []
    for mask in range(4):
        head = seq ^ mask
        piece = lax.dynamic_slice(cotangent[0], (0, ((3 * head) // 2) * HK), (PAIRS, WIN))
        grads.append(swap_seq(piece, mask) if mask else piece)

    joined_a, proj_a, columns = conv_chip(
        True, where, own, side, own_low, own_high, conv_weight, qkv_weight
    )
    far, proj_a = lax.optimization_barrier((far, proj_a))
    far_side = swap_seq(far, 1)
    joined_c, proj_c = conv_block(where, far, *far_halo[0], conv_weight, qkv_weight)
    far_side, proj_c = lax.optimization_barrier((far_side, proj_c))
    joined_d, proj_d = conv_block(where, far_side, *far_halo[1], conv_weight, qkv_weight)

    grad_a, grad_b, att_mine, att_side, att_b = attention(where, proj_a, proj_c, proj_d, grads)

    far_grad = swap_seq(grad_b, 2)
    side_grad = swap_seq(grad_a, 1)
    qkv_blocks = qkv_gradient(where, joined_a, joined_c, joined_d, grad_a, grad_b)
    far_grad, _ = lax.optimization_barrier((far_grad, qkv_blocks))
    qkv_blocks = over_plane(qkv_blocks)
    far_side_grad = swap_seq(far_grad, 1)
    conv_blocks = over_plane(
        conv_gradient(where, (grad_a, side_grad, far_grad, far_side_grad), qkv_weight, columns)
    )

    att_b, _ = lax.optimization_barrier((att_b, far_grad))
    att_far = swap_seq(att_b, 2)
    attended = attended_rows(
        where, (att_mine, swap_seq(att_side, 1), att_far[0], swap_seq(att_far[1], 1))
    )

    def finish(blocks):
        pieces = sum_stage(where, blocks)
        parts = [pieces[0]] + [shift_batch(pieces[d], 0, d) for d in (1, 2, 3)]
        summed = sum(part.astype(F32) for part in parts).astype(BF16)
        return [summed] + [swap_seq(summed, mask) for mask in (1, 2, 3)]

    grad_qkv = last_stage(
        last_qkv_kernel,
        where,
        finish(qkv_blocks),
        (QR, 1792),
        [pltpu.VMEM((HEADS, QR, HD), F32)],
    )
    conv_blocks, grad_qkv, attended = lax.optimization_barrier((conv_blocks, grad_qkv, attended))
    grad_conv = last_conv(over_column(spread_stage(conv_blocks)))
    return attended.reshape(1, PAIRS, HEADS * HV), grad_conv, grad_qkv


def solution(mesh):
    return jax.shard_map(
        shards,
        mesh=mesh,
        in_specs=(P("batch", "seq", None), P(), P(), P("batch", "seq", None)),
        out_specs=(P("batch", "seq", None), P("batch", None), P("batch", None)),
        check_vma=False,
    )
```

```python
import functools
import math

import jax
import jax.numpy as jnp
from jax import lax
from jax.experimental import pallas as pl
from jax.experimental.pallas import tpu as pltpu
from jax.sharding import PartitionSpec as P

HEADS = 4
HK = 128
HV = 192
WIN = 256
HD = 2 * HK + WIN
STEP = 4
C = 768
BINS = 512
PAIRS = 256
CHIP = 512
PAD = 8
CR = 36
QR = 24
QOFF = 112
JR = QOFF + 4 * QR
F32 = jnp.float32
BF16 = jnp.bfloat16

epsilon = 1e-06
temper = 1.0 / math.sqrt(HK)

VMEM = pl.BlockSpec(memory_space=pltpu.VMEM)
SMEM = pl.BlockSpec(memory_space=pltpu.SMEM)
HBM = pl.BlockSpec(memory_space=pltpu.HBM)


def params(mib):
    return pltpu.CompilerParams(vmem_limit_bytes=mib << 20)


def shape(dims, dtype=BF16):
    return jax.ShapeDtypeStruct(dims, dtype)


def cost(flops, nbytes):
    return pl.CostEstimate(flops=flops, bytes_accessed=nbytes, transcendentals=0)


def in_hbm(array):
    return pltpu.with_memory_space_constraint(array, pltpu.HBM)


def dot(a, b, ca=1, cb=0):
    return lax.dot_general(a, b, (((ca,), (cb,)), ((), ())), preferred_element_type=F32)


def swap_seq(block, mask):
    return lax.ppermute(block, "seq", [(i, i ^ mask) for i in range(4)])


def shift_batch(block, axis, distance):
    pairs = []
    for b in range(64):
        place = [b // 16, (b // 4) % 4, b % 4]
        place[axis] = (place[axis] + distance) % 4
        pairs.append((b, place[0] * 16 + place[1] * 4 + place[2]))
    return lax.ppermute(block, "batch", pairs)


def over_plane(blocks):
    groups = [[zh * 16 + place for place in range(16)] for zh in range(4)]
    return lax.all_to_all(
        blocks, "batch", split_axis=0, concat_axis=0, axis_index_groups=groups, tiled=True
    )


def sent(blocks, axis):
    return [blocks[0]] + [shift_batch(blocks[d], axis, d) for d in (1, 2, 3)]


def conv_kernel(keep, where, first, second, low, high, taps_hbm, weight_hbm, joined, proj, *refs):
    columns_hbm = refs[0] if keep else None
    act, stacked, bins, taps, weight, columns, sems, out_sem = refs[-8:]
    seq, core = where[0], where[1]
    loads = [pltpu.make_async_copy(taps_hbm, taps, sems.at[0])]
    for k, column in enumerate(
        (seq, HEADS + seq, 2 * HEADS + (3 * seq) // 2, 2 * HEADS + (3 * seq) // 2 + 1)
    ):
        source = weight_hbm.at[:, pl.ds(pl.multiple_of(column * HK, HK), HK)]
        loads.append(
            pltpu.make_async_copy(source, weight.at[:, k * HK : (k + 1) * HK], sems.at[1 + k])
        )
    for load in loads:
        load.start()
    for j in range(6):
        span = slice(j * 128, (j + 1) * 128)
        bins[j, 0:8, :] = low[:, span]
        here = pl.multiple_of(8 + core * BINS, 8)
        bins[j, pl.ds(here, BINS), :] = first[:, span].astype(F32)
        here = pl.multiple_of(8 + (1 - core) * BINS, 8)
        bins[j, pl.ds(here, BINS), :] = second[:, span].astype(F32)
        bins[j, 8 + 2 * BINS :, :] = high[:, span]

    def stream(parity, start, count):
        place = 8 + 2 * start + parity
        return jnp.concatenate(
            [bins[j, pl.ds(place, count, stride=2), :] for j in range(6)], axis=1
        )

    for parity in range(2):
        for start, count in ((-4, 4), (0, CHIP), (CHIP, 4)):
            act[PAD + start : PAD + start + count, :] = jax.nn.gelu(
                stream(parity, start, count), approximate=True
            )
        if keep and parity:
            pltpu.make_async_copy(columns, columns_hbm.at[0], out_sem).wait()
        for tap in range(3):
            start = PAD + (tap - 1) * (STEP // 2)
            rows = act[start : start + CHIP, :].astype(BF16)
            stacked[parity, :, tap * C : (tap + 1) * C] = rows
            if keep:
                columns[tap * C : (tap + 1) * C, :] = rows.T
        if keep:
            pltpu.make_async_copy(columns, columns_hbm.at[parity], out_sem).start()
        if parity == 0:
            loads[0].wait()
        out = stream(parity, 0, CHIP) + dot(stacked[parity], taps[...])
        joined[:, parity * C : (parity + 1) * C] = out.astype(BF16)
    for load in loads[1:]:
        load.wait()
    proj[...] = dot(joined[...], weight[...])
    if keep:
        pltpu.make_async_copy(columns, columns_hbm.at[1], out_sem).wait()


def conv_chip(keep, where, first, second, low, high, taps, weight):
    return pl.pallas_call(
        functools.partial(conv_kernel, keep),
        in_specs=[SMEM] + [VMEM] * 4 + [HBM] * 2,
        out_specs=[VMEM] * 2 + ([HBM] if keep else []),
        out_shape=[shape((CHIP, 2 * C)), shape((CHIP, HD), F32)]
        + ([pltpu.HBM((2, 3 * C, CHIP), BF16)] if keep else []),
        scratch_shapes=[
            pltpu.VMEM((CHIP + 2 * PAD, C), F32),
            pltpu.VMEM((2, CHIP, 3 * C), BF16),
            pltpu.VMEM((6, 2 * BINS + 16, 128), F32),
            pltpu.VMEM((3 * C, C), BF16),
            pltpu.VMEM((2 * C, HD), BF16),
            pltpu.VMEM((3 * C, CHIP) if keep else (8, 128), BF16),
            pltpu.SemaphoreType.DMA((5,)),
            pltpu.SemaphoreType.DMA,
        ],
        compiler_params=params(22),
        cost_estimate=cost(int(2 * 2 * 1024 * 3 * C * C) + 2 * CHIP * 2 * C * HD, 12 << 20)
        if keep
        else cost(1, 1),
        name="conv_own" if keep else "conv_far",
    )(where, first, second, low, high, in_hbm(taps), in_hbm(weight))


def unit(raw):
    return lax.rsqrt(jnp.mean(raw * raw, axis=-1, keepdims=True) + epsilon)


def unit_back(raw, grad_normed):
    factor = unit(raw)
    grad_f = grad_normed.astype(F32)
    inner = jnp.mean(grad_f * raw, axis=-1, keepdims=True)
    return (factor * grad_f - raw * factor * factor * factor * inner).astype(BF16)


def attention_kernel(
    where, proj_a, proj_b, g0, g1, g2, g3, grad_a, grad_b_hbm, att_mine, side_hbm, att_b_hbm,
    query, key, value, grad, key_sum, value_sum, att_side, att_b, grad_b, sems,
):
    core = where[1]
    lane = lax.broadcasted_iota(jnp.int32, (CHIP, WIN), 1)
    valid = (lane >= 64 * core) & (lane < 64 * core + HV)
    for part, proj in enumerate((proj_a, proj_b)):
        rows = slice(part * CHIP, (part + 1) * CHIP)
        raw = proj[:, :HK]
        query[rows, :] = (raw * unit(raw)).astype(BF16)
        raw = proj[:, HK : 2 * HK]
        key[rows, :] = (raw * unit(raw)).astype(BF16)
        value[rows, :] = jnp.where(valid, proj[:, 2 * HK :], 0.0).astype(BF16)
    for part, pair in enumerate(((g0, g1), (g2, g3))):
        for side in range(2):
            place = pl.multiple_of(part * CHIP + (core ^ side) * PAIRS, PAIRS)
            grad[pl.ds(place, PAIRS), :] = pair[side][...]
    keys, values = key[...], value[...]
    for tile in range(4):
        rows = slice(tile * PAIRS, (tile + 1) * PAIRS)
        local = slice((tile % 2) * PAIRS, (tile % 2 + 1) * PAIRS)
        queries, grads = query[rows, :], grad[rows, :]
        expo = jnp.exp(dot(queries, keys, 1, 1) * temper)
        probs = expo * (1.0 / jnp.sum(expo, axis=-1, keepdims=True))
        probs_b = probs.astype(BF16)
        attended = dot(probs_b, values).astype(BF16)
        if tile < 2:

            @pl.when(core == tile)
            def _():
                att_mine[...] = attended

            @pl.when(core != tile)
            def _():
                att_side[...] = attended
        else:
            att_b[core ^ (tile - 2)] = attended
        grad_value = dot(probs_b, grads, 0, 0)
        grad_probs = dot(grads, values, 1, 1)
        inner = jnp.sum(probs * grad_probs, axis=-1, keepdims=True)
        grad_scores = (probs * (grad_probs - inner) * temper).astype(BF16)
        grad_query = dot(grad_scores, keys).astype(BF16)
        grad_key = dot(grad_scores, queries, 0, 0)
        if tile:
            value_sum[...] += grad_value
            key_sum[...] += grad_key
        else:
            value_sum[...] = grad_value
            key_sum[...] = grad_key
        proj, out = (proj_a, grad_a) if tile < 2 else (proj_b, grad_b)
        out[local, :HK] = unit_back(proj[local, :HK], grad_query)
    stores = [
        pltpu.make_async_copy(att_side, side_hbm, sems.at[0]),
        pltpu.make_async_copy(att_b, att_b_hbm, sems.at[1]),
        pltpu.make_async_copy(grad_b, grad_b_hbm, sems.at[2]),
    ]
    stores[0].start()
    stores[1].start()
    for part, proj, out in ((1, proj_b, grad_b), (0, proj_a, grad_a)):
        rows = slice(part * CHIP, (part + 1) * CHIP)
        out[:, HK : 2 * HK] = unit_back(proj[:, HK : 2 * HK], key_sum[rows, :].astype(BF16))
        out[:, 2 * HK :] = jnp.where(valid, value_sum[rows, :], 0.0).astype(BF16)
        if part:
            stores[2].start()
    for store in stores:
        store.wait()


def attention(where, proj_a, proj_b, grads):
    return pl.pallas_call(
        attention_kernel,
        in_specs=[SMEM] + [VMEM] * 6,
        out_specs=[VMEM, HBM, VMEM, HBM, HBM],
        out_shape=[
            shape((CHIP, HD)),
            pltpu.HBM((CHIP, HD), BF16),
            shape((PAIRS, WIN)),
            pltpu.HBM((PAIRS, WIN), BF16),
            pltpu.HBM((2, PAIRS, WIN), BF16),
        ],
        scratch_shapes=[
            pltpu.VMEM((2 * CHIP, HK), BF16),
            pltpu.VMEM((2 * CHIP, HK), BF16),
            pltpu.VMEM((2 * CHIP, WIN), BF16),
            pltpu.VMEM((2 * CHIP, WIN), BF16),
            pltpu.VMEM((2 * CHIP, HK), F32),
            pltpu.VMEM((2 * CHIP, WIN), F32),
            pltpu.VMEM((PAIRS, WIN), BF16),
            pltpu.VMEM((2, PAIRS, WIN), BF16),
            pltpu.VMEM((CHIP, HD), BF16),
            pltpu.SemaphoreType.DMA((3,)),
        ],
        compiler_params=params(18),
        cost_estimate=cost(6 * 2 * 1024 * 1024 * 192, 6 << 20),
        name="attention",
    )(where, proj_a, proj_b, *grads)


def qkv_kernel(where, joined_a, joined_b, grad_a, grad_b, out_hbm, staged, sems):
    low = where[1] == 0
    for first in range(2):
        loose = []
        for zh in (first, first + 2):
            columns = slice(zh * 16 * QR, (zh + 1) * 16 * QR)
            table = dot(joined_a[:, columns], grad_a[...], 0, 0) + dot(
                joined_b[:, columns], grad_b[...], 0, 0
            )
            lower, upper = table[:, 256:384], table[:, 384:]
            panels = (table[:, :128], table[:, 128:256], jnp.where(low, lower, upper))
            loose.append(jnp.where(low, upper, lower))
            for k, panel in enumerate(panels):
                rows = panel.astype(BF16)
                span = slice((4 * k + zh) * QR, (4 * k + zh + 1) * QR)
                for place in range(16):
                    staged[place, span, :] = rows[place * QR : (place + 1) * QR, :]
        turned = [pltpu.roll(half, 64, 1) for half in loose]
        rows = (jnp.where(low, loose[0], turned[0]) + jnp.where(low, turned[1], loose[1])).astype(
            BF16
        )
        span = slice((12 + first) * QR, (13 + first) * QR)
        for place in range(16):
            staged[place, span, :] = rows[place * QR : (place + 1) * QR, :]
    store = pltpu.make_async_copy(staged, out_hbm, sems)
    store.start()
    store.wait()


def qkv_gradient(where, joined_a, joined_b, grad_a, grad_b):
    return pl.pallas_call(
        qkv_kernel,
        in_specs=[SMEM] + [VMEM] * 4,
        out_specs=HBM,
        out_shape=pltpu.HBM((16, 14 * QR, 128), BF16),
        scratch_shapes=[
            pltpu.VMEM((16, 14 * QR, 128), BF16),
            pltpu.SemaphoreType.DMA,
        ],
        compiler_params=params(14),
        cost_estimate=cost(2 * 1536 * 1024 * HD, 6 << 20),
        name="qkv_gradient",
    )(where, joined_a, joined_b, grad_a, grad_b)


def value_units(place, heads):
    place(0, heads[0][0])
    place(1, heads[0][1] + heads[1][0])
    place(2, heads[1][1])
    place(3, heads[2][0])
    place(4, heads[2][1] + heads[3][0])
    place(5, heads[3][1])


def conv_gradient_kernel(where, g0, g1, g2, g3, weight_hbm, columns_hbm, *refs):
    out_x, out_y = refs[:4], refs[4:8]
    by_head, natural, weight, columns, table, pieces, sems = refs[8:]
    seq, core, x, y = where[0], where[1], where[3], where[4]
    half = C // 2
    loads = []
    for p in range(2):
        source = weight_hbm.at[pl.ds(pl.multiple_of(p * C + core * half, half), half), :]
        loads.append(
            pltpu.make_async_copy(source, weight.at[p * half : (p + 1) * half, :], sems.at[p])
        )
    for p in range(2):
        loads.append(pltpu.make_async_copy(columns_hbm.at[p], columns.at[p], sems.at[2 + p]))
    for load in loads:
        load.start()
    for mask, ref in enumerate((g0, g1, g2, g3)):
        by_head[seq ^ mask] = ref[...]
    for h in range(HEADS):
        natural[:, h * HK : (h + 1) * HK] = by_head[h, :, :HK]
        natural[:, (HEADS + h) * HK : (HEADS + h + 1) * HK] = by_head[h, :, HK : 2 * HK]

    def place(index, rows):
        natural[:, (2 * HEADS + index) * HK : (2 * HEADS + index + 1) * HK] = rows

    value_units(
        place, [[by_head[h, :, (2 + k) * HK : (3 + k) * HK] for k in range(2)] for h in range(HEADS)]
    )
    loads[0].wait()
    loads[1].wait()
    hidden = dot(natural[...], weight[...], 1, 1).astype(BF16)
    loads[2].wait()
    loads[3].wait()
    block = 4 * CR
    for zh in range(4):
        rows = slice(zh * 4 * block, (zh + 1) * 4 * block)
        table[...] = dot(columns[0, rows, :], hidden[:, :half]) + dot(
            columns[1, rows, :], hidden[:, half:]
        )
        if zh < 2:
            for d in range(4):
                begin = pl.multiple_of(((x + d) % 4) * block, 8)
                out_x[d][zh] = table[pl.ds(begin, block), :].astype(BF16)
        else:
            for xx in range(4):
                chunk = table[xx * block : (xx + 1) * block, :]
                for yy in range(4):
                    pieces[(yy - y + 4) % 4, zh - 2, xx * CR : (xx + 1) * CR, :] = chunk[
                        yy * CR : (yy + 1) * CR, :
                    ]
    for d in range(4):
        out_y[d][...] = pieces[d].astype(BF16)


def conv_gradient(where, grads, weight, columns):
    return pl.pallas_call(
        conv_gradient_kernel,
        in_specs=[SMEM] + [VMEM] * 4 + [HBM] * 2,
        out_specs=[VMEM] * 8,
        out_shape=[shape((2, 4 * CR, C // 2))] * 8,
        scratch_shapes=[
            pltpu.VMEM((HEADS, CHIP, HD), BF16),
            pltpu.VMEM((CHIP, 1792), BF16),
            pltpu.VMEM((C, 1792), BF16),
            pltpu.VMEM((2, 3 * C, CHIP), BF16),
            pltpu.VMEM((16 * CR, C // 2), F32),
            pltpu.VMEM((4, 2, 4 * CR, C // 2), F32),
            pltpu.SemaphoreType.DMA((4,)),
        ],
        compiler_params=params(20),
        cost_estimate=cost(int(0.3 * (2 * CHIP * 1792 * C + 2 * 1024 * 3 * C * C // 2)), 1 << 20),
        name="conv_gradient",
    )(where, *grads, in_hbm(weight), in_hbm(columns))


def total(refs):
    out = refs[0][...].astype(F32)
    for ref in refs[1:]:
        out = out + ref[...].astype(F32)
    return out


def second_kernel(where, *refs):
    outs, pieces = refs[8:16], refs[16]
    for half, me in enumerate((where[4], where[3])):
        summed = total(refs[4 * half : 4 * half + 4])
        for k in range(4):
            pieces[(k - me + 4) % 4] = summed[:, k * CR : (k + 1) * CR, :]
        for d in range(4):
            outs[4 * half + d][...] = pieces[d].astype(BF16)


def second_stage(where, blocks):
    dims = (2, CR, C // 2)
    return pl.pallas_call(
        second_kernel,
        in_specs=[SMEM] + [VMEM] * 8,
        out_specs=[VMEM] * 8,
        out_shape=[shape(dims)] * 8,
        scratch_shapes=[pltpu.VMEM((4, *dims), F32)],
        compiler_params=params(10),
        name="second_stage",
    )(where, *blocks)


def sum_kernel(where, blocks, out):
    low = where[1] == 0
    rows = blocks[0].astype(F32)
    for place in range(1, 16):
        rows = rows + blocks[place].astype(F32)
    count = 4 * QR
    full, loose = rows[2 * count : 3 * count, :], rows[3 * count :, :]
    turned = pltpu.roll(loose, 64, 1)
    half = jnp.concatenate([jnp.where(low, loose, turned), jnp.where(low, turned, loose)])
    lane = lax.broadcasted_iota(jnp.int32, half.shape, 1)
    half = jnp.where((lane < 64) == low, half, 0.0)
    out[:, :128] = rows[:count, :]
    out[:, 128:256] = rows[count : 2 * count, :]
    out[:, 256:384] = jnp.where(low, full, half)
    out[:, 384:] = jnp.where(low, half, full)


def sum_stage(where, blocks):
    return pl.pallas_call(
        sum_kernel,
        in_specs=[SMEM, VMEM],
        out_specs=VMEM,
        out_shape=shape((4 * QR, HD), F32),
        compiler_params=params(8),
        name="sum_stage",
    )(where, blocks)


def joint_kernel(where, qkv, *refs):
    conv, outs, pieces = refs[:8], refs[8:12], refs[12]
    halves = [total(conv[:4]), total(conv[4:])]
    for zh in range(4):
        for j in range(3):
            pieces[zh, j * CR : (j + 1) * CR, :] = halves[zh // 2][
                zh % 2, :, j * 128 : (j + 1) * 128
            ]
        pieces[zh, 3 * CR : QOFF, :] = jnp.zeros((QOFF - 3 * CR, 128), F32)
        for j in range(4):
            pieces[zh, QOFF + j * QR : QOFF + (j + 1) * QR, :] = qkv[
                zh * QR : (zh + 1) * QR, j * 128 : (j + 1) * 128
            ]
    for d in range(4):
        outs[d][...] = pieces[(where[2] + d) % 4].astype(BF16)


def joint_stage(where, qkv, conv):
    return pl.pallas_call(
        joint_kernel,
        in_specs=[SMEM] + [VMEM] * 9,
        out_specs=[VMEM] * 4,
        out_shape=[shape((JR, 128))] * 4,
        scratch_shapes=[pltpu.VMEM((4, JR, 128), F32)],
        compiler_params=params(6),
        name="joint_stage",
    )(where, qkv, *conv)


def last_kernel(where, r0, r1, r2, r3, grad_conv, grad_qkv, by_head):
    seq, core = where[0], where[1]
    parts = [ref[...].astype(F32) for ref in (r0, r1, r2, r3)]
    here = parts[0] + parts[2]
    there = parts[1] + parts[3]
    low = jnp.where(core == 0, here, there)
    high = jnp.where(core == 0, there, here)
    for j in range(3):
        span = slice(j * CR, (j + 1) * CR)
        grad_conv[:, j * 128 : (j + 1) * 128] = low[span, :]
        grad_conv[:, (3 + j) * 128 : (4 + j) * 128] = high[span, :]
    for mask in range(4):
        by_head[seq ^ mask] = parts[mask][QOFF:, :]

    def place(index, rows):
        grad_qkv[:, index * 128 : (index + 1) * 128] = rows

    for h in range(HEADS):
        place(h, by_head[h, :QR, :])
        place(HEADS + h, by_head[h, QR : 2 * QR, :])
    value_units(
        lambda index, rows: place(2 * HEADS + index, rows),
        [[by_head[h, (2 + k) * QR : (3 + k) * QR, :] for k in range(2)] for h in range(HEADS)],
    )


def last_stage(where, parts):
    return pl.pallas_call(
        last_kernel,
        in_specs=[SMEM] + [VMEM] * 4,
        out_specs=[VMEM] * 2,
        out_shape=[shape((CR, C), F32), shape((QR, 1792), F32)],
        scratch_shapes=[pltpu.VMEM((HEADS, 4 * QR, 128), F32)],
        compiler_params=params(4),
        name="last_stage",
    )(where, *parts)


def attended_kernel(where, a0, a1, a2, a3, out, by_head):
    for mask, ref in enumerate((a0, a1, a2, a3)):
        by_head[where[0] ^ mask] = ref[...]

    def place(index, rows):
        out[:, index * 128 : (index + 1) * 128] = rows

    value_units(
        place, [[by_head[h, :, k * HK : (k + 1) * HK] for k in range(2)] for h in range(HEADS)]
    )


def attended_rows(where, parts):
    return pl.pallas_call(
        attended_kernel,
        in_specs=[SMEM] + [VMEM] * 4,
        out_specs=VMEM,
        out_shape=shape((PAIRS, C)),
        scratch_shapes=[pltpu.VMEM((HEADS, PAIRS, WIN), BF16)],
        compiler_params=params(4),
        name="attended_rows",
    )(where, *parts)


def shards(embedded, conv_weight, qkv_weight, cotangent):
    own = embedded[0]
    seq = lax.axis_index("seq")
    batch = lax.axis_index("batch")
    core, chip = seq % 2, seq // 2
    where = jnp.stack([seq, core, batch // 16, (batch // 4) % 4, batch % 4]).astype(jnp.int32)

    edges = jnp.concatenate([own[:8], own[-8:]])
    own, edges = lax.optimization_barrier((own, edges))
    edge_same, edge_other = swap_seq(edges, 2), swap_seq(edges, 3)
    side = swap_seq(own, 1)
    far = swap_seq(own, 2)
    zero = jnp.zeros((8, C), F32)
    first = lambda a, b: jnp.where(core == 0, a, b)[:8].astype(F32)
    last = lambda a, b: jnp.where(core == 0, b, a)[8:].astype(F32)
    side_edges = jnp.concatenate([side[:8], side[-8:]])
    own_low = jnp.where(chip == 1, last(edge_same, edge_other), zero)
    own_high = jnp.where(chip == 0, first(edge_same, edge_other), zero)
    far_low = jnp.where(chip == 0, last(edges, side_edges), zero)
    far_high = jnp.where(chip == 1, first(edges, side_edges), zero)

    grads = []
    for mask in range(4):
        head = seq ^ mask
        piece = lax.dynamic_slice(cotangent[0], (0, ((3 * head) // 2) * HK), (PAIRS, WIN))
        grads.append(swap_seq(piece, mask) if mask else piece)

    joined_a, proj_a, columns = conv_chip(
        True, where, own, side, own_low, own_high, conv_weight, qkv_weight
    )
    far, proj_a = lax.optimization_barrier((far, proj_a))
    far_side = swap_seq(far, 1)
    joined_b, proj_b = conv_chip(
        False, where, far, far_side, far_low, far_high, conv_weight, qkv_weight
    )

    grad_a, grad_b, att_mine, att_side, att_b = attention(where, proj_a, proj_b, grads)

    far_grad = swap_seq(grad_b, 2)
    side_grad = swap_seq(grad_a, 1)
    qkv_blocks = qkv_gradient(where, joined_a, joined_b, grad_a, grad_b)
    far_grad, _ = lax.optimization_barrier((far_grad, qkv_blocks))
    qkv_blocks = over_plane(qkv_blocks)
    far_side_grad = swap_seq(far_grad, 1)
    conv_blocks = conv_gradient(
        where, (grad_a, side_grad, far_grad, far_side_grad), qkv_weight, columns
    )

    att_b, _ = lax.optimization_barrier((att_b, far_grad))
    att_far = swap_seq(att_b, 2)
    attended = attended_rows(
        where, (att_mine, swap_seq(att_side, 1), att_far[0], swap_seq(att_far[1], 1))
    )

    conv_blocks = sent(conv_blocks[:4], 1) + sent(conv_blocks[4:], 2)
    qkv_sum = sum_stage(where, qkv_blocks)
    conv_blocks, qkv_sum, attended = lax.optimization_barrier((conv_blocks, qkv_sum, attended))
    conv_blocks = second_stage(where, conv_blocks)
    conv_blocks = sent(conv_blocks[:4], 2) + sent(conv_blocks[4:], 1)
    parts = sent(joint_stage(where, qkv_sum, conv_blocks), 0)
    summed = sum(part.astype(F32) for part in parts).astype(BF16)
    grad_conv, grad_qkv = last_stage(
        where, [summed] + [swap_seq(summed, mask) for mask in (1, 2, 3)]
    )
    return attended.reshape(1, PAIRS, HEADS * HV), grad_conv, grad_qkv


def solution(mesh):
    return jax.shard_map(
        shards,
        mesh=mesh,
        in_specs=(P("batch", "seq", None), P(), P(), P("batch", "seq", None)),
        out_specs=(P("batch", "seq", None), P("batch", None), P("batch", None)),
        check_vma=False,
    )
```

```python
import functools
import math

import jax
import jax.numpy as jnp
from jax import lax
from jax.experimental import pallas as pl
from jax.experimental.pallas import tpu as pltpu
from jax.sharding import PartitionSpec as P

HEADS = 4
HK = 128
HV = 192
WIN = 256
HD = 2 * HK + WIN
STEP = 4
C = 768
BINS = 512
PAIRS = 256
CHIP = 512
PAD = 8
CR = 36
QR = 24
QOFF = 112
JR = QOFF + 4 * QR
F32 = jnp.float32
BF16 = jnp.bfloat16

epsilon = 1e-06
temper = 1.0 / math.sqrt(HK)

VMEM = pl.BlockSpec(memory_space=pltpu.VMEM)
SMEM = pl.BlockSpec(memory_space=pltpu.SMEM)
HBM = pl.BlockSpec(memory_space=pltpu.HBM)


def params(mib):
    return pltpu.CompilerParams(vmem_limit_bytes=mib << 20)


def shape(dims, dtype=BF16):
    return jax.ShapeDtypeStruct(dims, dtype)


def cost(flops, nbytes):
    return pl.CostEstimate(flops=flops, bytes_accessed=nbytes, transcendentals=0)


def in_hbm(array):
    return pltpu.with_memory_space_constraint(array, pltpu.HBM)


def dot(a, b, ca=1, cb=0):
    return lax.dot_general(a, b, (((ca,), (cb,)), ((), ())), preferred_element_type=F32)


def swap_seq(block, mask):
    return lax.ppermute(block, "seq", [(i, i ^ mask) for i in range(4)])


def shift_batch(block, axis, distance):
    pairs = []
    for b in range(64):
        place = [b // 16, (b // 4) % 4, b % 4]
        place[axis] = (place[axis] + distance) % 4
        pairs.append((b, place[0] * 16 + place[1] * 4 + place[2]))
    return lax.ppermute(block, "batch", pairs)


def over_plane(blocks):
    groups = [[zh * 16 + place for place in range(16)] for zh in range(4)]
    return lax.all_to_all(
        blocks, "batch", split_axis=0, concat_axis=0, axis_index_groups=groups, tiled=True
    )


def sent(blocks, axis):
    return [blocks[0]] + [shift_batch(blocks[d], axis, d) for d in (1, 2, 3)]


def conv_kernel(keep, where, first, second, low, high, taps_hbm, weight_hbm, joined, proj, *refs):
    columns_hbm = refs[0] if keep else None
    act, stacked, bins, taps, weight, columns, sems, out_sem = refs[-8:]
    seq, core = where[0], where[1]
    loads = [pltpu.make_async_copy(taps_hbm, taps, sems.at[0])]
    for k, column in enumerate(
        (seq, HEADS + seq, 2 * HEADS + (3 * seq) // 2, 2 * HEADS + (3 * seq) // 2 + 1)
    ):
        source = weight_hbm.at[:, pl.ds(pl.multiple_of(column * HK, HK), HK)]
        loads.append(
            pltpu.make_async_copy(source, weight.at[:, k * HK : (k + 1) * HK], sems.at[1 + k])
        )
    for load in loads:
        load.start()
    for j in range(6):
        span = slice(j * 128, (j + 1) * 128)
        bins[j, 0:8, :] = low[:, span]
        here = pl.multiple_of(8 + core * BINS, 8)
        bins[j, pl.ds(here, BINS), :] = first[:, span].astype(F32)
        here = pl.multiple_of(8 + (1 - core) * BINS, 8)
        bins[j, pl.ds(here, BINS), :] = second[:, span].astype(F32)
        bins[j, 8 + 2 * BINS :, :] = high[:, span]

    def stream(parity, start, count):
        place = 8 + 2 * start + parity
        return jnp.concatenate(
            [bins[j, pl.ds(place, count, stride=2), :] for j in range(6)], axis=1
        )

    for parity in range(2):
        for start, count in ((-4, 4), (0, CHIP), (CHIP, 4)):
            act[PAD + start : PAD + start + count, :] = jax.nn.gelu(
                stream(parity, start, count), approximate=True
            )
        if keep and parity:
            pltpu.make_async_copy(columns, columns_hbm.at[0], out_sem).wait()
        for tap in range(3):
            start = PAD + (tap - 1) * (STEP // 2)
            rows = act[start : start + CHIP, :].astype(BF16)
            stacked[parity, :, tap * C : (tap + 1) * C] = rows
            if keep:
                columns[tap * C : (tap + 1) * C, :] = rows.T
        if keep:
            pltpu.make_async_copy(columns, columns_hbm.at[parity], out_sem).start()
        if parity == 0:
            loads[0].wait()
        out = stream(parity, 0, CHIP) + dot(stacked[parity], taps[...])
        joined[:, parity * C : (parity + 1) * C] = out.astype(BF16)
    for load in loads[1:]:
        load.wait()
    proj[...] = dot(joined[...], weight[...])
    if keep:
        pltpu.make_async_copy(columns, columns_hbm.at[1], out_sem).wait()


def conv_chip(keep, where, first, second, low, high, taps, weight):
    return pl.pallas_call(
        functools.partial(conv_kernel, keep),
        in_specs=[SMEM] + [VMEM] * 4 + [HBM] * 2,
        out_specs=[VMEM] * 2 + ([HBM] if keep else []),
        out_shape=[shape((CHIP, 2 * C)), shape((CHIP, HD), F32)]
        + ([pltpu.HBM((2, 3 * C, CHIP), BF16)] if keep else []),
        scratch_shapes=[
            pltpu.VMEM((CHIP + 2 * PAD, C), F32),
            pltpu.VMEM((2, CHIP, 3 * C), BF16),
            pltpu.VMEM((6, 2 * BINS + 16, 128), F32),
            pltpu.VMEM((3 * C, C), BF16),
            pltpu.VMEM((2 * C, HD), BF16),
            pltpu.VMEM((3 * C, CHIP) if keep else (8, 128), BF16),
            pltpu.SemaphoreType.DMA((5,)),
            pltpu.SemaphoreType.DMA,
        ],
        compiler_params=params(22),
        cost_estimate=cost(int(2 * 2 * 1024 * 3 * C * C) + 2 * CHIP * 2 * C * HD, 12 << 20)
        if keep
        else cost(1, 1),
        name="conv_own" if keep else "conv_far",
    )(where, first, second, low, high, in_hbm(taps), in_hbm(weight))


def unit(raw):
    return lax.rsqrt(jnp.mean(raw * raw, axis=-1, keepdims=True) + epsilon)


def unit_back(raw, grad_normed):
    factor = unit(raw)
    grad_f = grad_normed.astype(F32)
    inner = jnp.mean(grad_f * raw, axis=-1, keepdims=True)
    return (factor * grad_f - raw * factor * factor * factor * inner).astype(BF16)


def attention_kernel(
    where, proj_a, proj_b, g0, g1, g2, g3, grad_a, grad_b_hbm, att_mine, side_hbm, att_b_hbm,
    query, key, value, grad, key_sum, value_sum, att_side, att_b, grad_b, sems,
):
    core = where[1]
    lane = lax.broadcasted_iota(jnp.int32, (CHIP, WIN), 1)
    valid = (lane >= 64 * core) & (lane < 64 * core + HV)
    for part, proj in enumerate((proj_a, proj_b)):
        rows = slice(part * CHIP, (part + 1) * CHIP)
        raw = proj[:, :HK]
        query[rows, :] = (raw * unit(raw)).astype(BF16)
        raw = proj[:, HK : 2 * HK]
        key[rows, :] = (raw * unit(raw)).astype(BF16)
        value[rows, :] = jnp.where(valid, proj[:, 2 * HK :], 0.0).astype(BF16)
    for part, pair in enumerate(((g0, g1), (g2, g3))):
        for side in range(2):
            place = pl.multiple_of(part * CHIP + (core ^ side) * PAIRS, PAIRS)
            grad[pl.ds(place, PAIRS), :] = pair[side][...]
    keys, values = key[...], value[...]
    for tile in range(4):
        rows = slice(tile * PAIRS, (tile + 1) * PAIRS)
        local = slice((tile % 2) * PAIRS, (tile % 2 + 1) * PAIRS)
        queries, grads = query[rows, :], grad[rows, :]
        expo = jnp.exp(dot(queries, keys, 1, 1) * temper)
        probs = expo * (1.0 / jnp.sum(expo, axis=-1, keepdims=True))
        probs_b = probs.astype(BF16)
        attended = dot(probs_b, values).astype(BF16)
        if tile < 2:

            @pl.when(core == tile)
            def _():
                att_mine[...] = attended

            @pl.when(core != tile)
            def _():
                att_side[...] = attended
        else:
            att_b[core ^ (tile - 2)] = attended
        grad_value = dot(probs_b, grads, 0, 0)
        grad_probs = dot(grads, values, 1, 1)
        inner = jnp.sum(probs * grad_probs, axis=-1, keepdims=True)
        grad_scores = (probs * (grad_probs - inner) * temper).astype(BF16)
        grad_query = dot(grad_scores, keys).astype(BF16)
        grad_key = dot(grad_scores, queries, 0, 0)
        if tile:
            value_sum[...] += grad_value
            key_sum[...] += grad_key
        else:
            value_sum[...] = grad_value
            key_sum[...] = grad_key
        proj, out = (proj_a, grad_a) if tile < 2 else (proj_b, grad_b)
        out[local, :HK] = unit_back(proj[local, :HK], grad_query)
    stores = [
        pltpu.make_async_copy(att_side, side_hbm, sems.at[0]),
        pltpu.make_async_copy(att_b, att_b_hbm, sems.at[1]),
        pltpu.make_async_copy(grad_b, grad_b_hbm, sems.at[2]),
    ]
    stores[0].start()
    stores[1].start()
    for part, proj, out in ((1, proj_b, grad_b), (0, proj_a, grad_a)):
        rows = slice(part * CHIP, (part + 1) * CHIP)
        out[:, HK : 2 * HK] = unit_back(proj[:, HK : 2 * HK], key_sum[rows, :].astype(BF16))
        out[:, 2 * HK :] = jnp.where(valid, value_sum[rows, :], 0.0).astype(BF16)
        if part:
            stores[2].start()
    for store in stores:
        store.wait()


def attention(where, proj_a, proj_b, grads):
    return pl.pallas_call(
        attention_kernel,
        in_specs=[SMEM] + [VMEM] * 6,
        out_specs=[VMEM, HBM, VMEM, HBM, HBM],
        out_shape=[
            shape((CHIP, HD)),
            pltpu.HBM((CHIP, HD), BF16),
            shape((PAIRS, WIN)),
            pltpu.HBM((PAIRS, WIN), BF16),
            pltpu.HBM((2, PAIRS, WIN), BF16),
        ],
        scratch_shapes=[
            pltpu.VMEM((2 * CHIP, HK), BF16),
            pltpu.VMEM((2 * CHIP, HK), BF16),
            pltpu.VMEM((2 * CHIP, WIN), BF16),
            pltpu.VMEM((2 * CHIP, WIN), BF16),
            pltpu.VMEM((2 * CHIP, HK), F32),
            pltpu.VMEM((2 * CHIP, WIN), F32),
            pltpu.VMEM((PAIRS, WIN), BF16),
            pltpu.VMEM((2, PAIRS, WIN), BF16),
            pltpu.VMEM((CHIP, HD), BF16),
            pltpu.SemaphoreType.DMA((3,)),
        ],
        compiler_params=params(20),
        cost_estimate=cost(6 * 2 * 1024 * 1024 * 192, 6 << 20),
        name="attention",
    )(where, proj_a, proj_b, *grads)


def qkv_kernel(
    where, joined_a, joined_b, grad_a, grad_b_hbm, out_hbm, staged, grad_b, load_sem, sems
):
    low = where[1] == 0
    load = pltpu.make_async_copy(grad_b_hbm, grad_b, load_sem)
    load.start()
    stores = []
    for first in range(2):
        loose = []
        group = 7 * first
        for zh in (first, first + 2):
            columns = slice(zh * 16 * QR, (zh + 1) * 16 * QR)
            table = dot(joined_a[:, columns], grad_a[...], 0, 0)
            if zh == 0:
                load.wait()
            table = table + dot(joined_b[:, columns], grad_b[...], 0, 0)
            lower, upper = table[:, 256:384], table[:, 384:]
            panels = (table[:, :128], table[:, 128:256], jnp.where(low, lower, upper))
            loose.append(jnp.where(low, upper, lower))
            for k, panel in enumerate(panels):
                rows = panel.astype(BF16)
                start = (group + 2 * k + zh // 2) * QR
                for place in range(16):
                    staged[place, start : start + QR, :] = rows[place * QR : (place + 1) * QR, :]
        turned = [pltpu.roll(half, 64, 1) for half in loose]
        rows = (jnp.where(low, loose[0], turned[0]) + jnp.where(low, turned[1], loose[1])).astype(
            BF16
        )
        start = (group + 6) * QR
        for place in range(16):
            staged[place, start : start + QR, :] = rows[place * QR : (place + 1) * QR, :]
        span = slice(group * QR, (group + 7) * QR)
        stores.append(
            pltpu.make_async_copy(staged.at[:, span, :], out_hbm.at[:, span, :], sems.at[first])
        )
        stores[-1].start()
    for store in stores:
        store.wait()


def qkv_gradient(where, joined_a, joined_b, grad_a, grad_b):
    return pl.pallas_call(
        qkv_kernel,
        in_specs=[SMEM] + [VMEM] * 3 + [HBM],
        out_specs=HBM,
        out_shape=pltpu.HBM((16, 14 * QR, 128), BF16),
        scratch_shapes=[
            pltpu.VMEM((16, 14 * QR, 128), BF16),
            pltpu.VMEM((CHIP, HD), BF16),
            pltpu.SemaphoreType.DMA,
            pltpu.SemaphoreType.DMA((2,)),
        ],
        compiler_params=params(14),
        cost_estimate=cost(2 * 1536 * 1024 * HD, 6 << 20),
        name="qkv_gradient",
    )(where, joined_a, joined_b, grad_a, in_hbm(grad_b))


def value_units(place, heads):
    place(0, heads[0][0])
    place(1, heads[0][1] + heads[1][0])
    place(2, heads[1][1])
    place(3, heads[2][0])
    place(4, heads[2][1] + heads[3][0])
    place(5, heads[3][1])


def conv_gradient_kernel(where, g0, g1, g2, g3, weight_hbm, columns_hbm, *refs):
    out_x, out_y = refs[:4], refs[4:8]
    by_head, natural, weight, columns, table, pieces, sems = refs[8:]
    seq, core, x, y = where[0], where[1], where[3], where[4]
    half = C // 2
    loads = []
    for p in range(2):
        source = weight_hbm.at[pl.ds(pl.multiple_of(p * C + core * half, half), half), :]
        loads.append(
            pltpu.make_async_copy(source, weight.at[p * half : (p + 1) * half, :], sems.at[p])
        )
    for p in range(2):
        loads.append(pltpu.make_async_copy(columns_hbm.at[p], columns.at[p], sems.at[2 + p]))
    for load in loads:
        load.start()
    for mask, ref in enumerate((g0, g1, g2, g3)):
        by_head[seq ^ mask] = ref[...]
    for h in range(HEADS):
        natural[:, h * HK : (h + 1) * HK] = by_head[h, :, :HK]
        natural[:, (HEADS + h) * HK : (HEADS + h + 1) * HK] = by_head[h, :, HK : 2 * HK]

    def place(index, rows):
        natural[:, (2 * HEADS + index) * HK : (2 * HEADS + index + 1) * HK] = rows

    value_units(
        place, [[by_head[h, :, (2 + k) * HK : (3 + k) * HK] for k in range(2)] for h in range(HEADS)]
    )
    loads[0].wait()
    loads[1].wait()
    hidden = dot(natural[...], weight[...], 1, 1).astype(BF16)
    loads[2].wait()
    loads[3].wait()
    block = 4 * CR
    for zh in range(4):
        rows = slice(zh * 4 * block, (zh + 1) * 4 * block)
        table[...] = dot(columns[0, rows, :], hidden[:, :half]) + dot(
            columns[1, rows, :], hidden[:, half:]
        )
        if zh < 2:
            for d in range(4):
                begin = pl.multiple_of(((x + d) % 4) * block, 8)
                out_x[d][zh] = table[pl.ds(begin, block), :].astype(BF16)
        else:
            for xx in range(4):
                chunk = table[xx * block : (xx + 1) * block, :]
                for yy in range(4):
                    pieces[(yy - y + 4) % 4, zh - 2, xx * CR : (xx + 1) * CR, :] = chunk[
                        yy * CR : (yy + 1) * CR, :
                    ]
    for d in range(4):
        out_y[d][...] = pieces[d].astype(BF16)


def conv_gradient(where, grads, weight, columns):
    return pl.pallas_call(
        conv_gradient_kernel,
        in_specs=[SMEM] + [VMEM] * 4 + [HBM] * 2,
        out_specs=[VMEM] * 8,
        out_shape=[shape((2, 4 * CR, C // 2))] * 8,
        scratch_shapes=[
            pltpu.VMEM((HEADS, CHIP, HD), BF16),
            pltpu.VMEM((CHIP, 1792), BF16),
            pltpu.VMEM((C, 1792), BF16),
            pltpu.VMEM((2, 3 * C, CHIP), BF16),
            pltpu.VMEM((16 * CR, C // 2), F32),
            pltpu.VMEM((4, 2, 4 * CR, C // 2), F32),
            pltpu.SemaphoreType.DMA((4,)),
        ],
        compiler_params=params(20),
        cost_estimate=cost(int(0.3 * (2 * CHIP * 1792 * C + 2 * 1024 * 3 * C * C // 2)), 1 << 20),
        name="conv_gradient",
    )(where, *grads, in_hbm(weight), in_hbm(columns))


def total(refs):
    out = refs[0][...].astype(F32)
    for ref in refs[1:]:
        out = out + ref[...].astype(F32)
    return out


def second_kernel(where, *refs):
    outs, pieces = refs[8:16], refs[16]
    for half, me in enumerate((where[4], where[3])):
        summed = total(refs[4 * half : 4 * half + 4])
        for k in range(4):
            pieces[(k - me + 4) % 4] = summed[:, k * CR : (k + 1) * CR, :]
        for d in range(4):
            outs[4 * half + d][...] = pieces[d].astype(BF16)


def second_stage(where, blocks):
    dims = (2, CR, C // 2)
    return pl.pallas_call(
        second_kernel,
        in_specs=[SMEM] + [VMEM] * 8,
        out_specs=[VMEM] * 8,
        out_shape=[shape(dims)] * 8,
        scratch_shapes=[pltpu.VMEM((4, *dims), F32)],
        compiler_params=params(10),
        name="second_stage",
    )(where, *blocks)


def sum_kernel(where, blocks, out):
    low = where[1] == 0
    rows = blocks[0].astype(F32)
    for place in range(1, 16):
        rows = rows + blocks[place].astype(F32)
    lane = lax.broadcasted_iota(jnp.int32, (QR, 128), 1)
    valid = (lane < 64) == low
    take = lambda group: rows[group * QR : (group + 1) * QR, :]
    for zh in range(4):
        group = 7 * (zh % 2)
        span = slice(zh * QR, (zh + 1) * QR)
        full, loose = take(group + 4 + zh // 2), take(group + 6)
        turned = pltpu.roll(loose, 64, 1)
        half = jnp.where(low, loose, turned) if zh < 2 else jnp.where(low, turned, loose)
        half = jnp.where(valid, half, 0.0)
        out[span, :128] = take(group + zh // 2)
        out[span, 128:256] = take(group + 2 + zh // 2)
        out[span, 256:384] = jnp.where(low, full, half)
        out[span, 384:] = jnp.where(low, half, full)


def sum_stage(where, blocks):
    return pl.pallas_call(
        sum_kernel,
        in_specs=[SMEM, VMEM],
        out_specs=VMEM,
        out_shape=shape((4 * QR, HD), F32),
        compiler_params=params(8),
        name="sum_stage",
    )(where, blocks)


def joint_kernel(where, qkv, *refs):
    conv, outs, pieces = refs[:8], refs[8:12], refs[12]
    halves = [total(conv[:4]), total(conv[4:])]
    for zh in range(4):
        for j in range(3):
            pieces[zh, j * CR : (j + 1) * CR, :] = halves[zh // 2][
                zh % 2, :, j * 128 : (j + 1) * 128
            ]
        pieces[zh, 3 * CR : QOFF, :] = jnp.zeros((QOFF - 3 * CR, 128), F32)
        for j in range(4):
            pieces[zh, QOFF + j * QR : QOFF + (j + 1) * QR, :] = qkv[
                zh * QR : (zh + 1) * QR, j * 128 : (j + 1) * 128
            ]
    for d in range(4):
        outs[d][...] = pieces[(where[2] + d) % 4].astype(BF16)


def joint_stage(where, qkv, conv):
    return pl.pallas_call(
        joint_kernel,
        in_specs=[SMEM] + [VMEM] * 9,
        out_specs=[VMEM] * 4,
        out_shape=[shape((JR, 128))] * 4,
        scratch_shapes=[pltpu.VMEM((4, JR, 128), F32)],
        compiler_params=params(6),
        name="joint_stage",
    )(where, qkv, *conv)


def last_kernel(where, r0, r1, r2, r3, grad_conv, grad_qkv, by_head):
    seq, core = where[0], where[1]
    parts = [ref[...].astype(F32) for ref in (r0, r1, r2, r3)]
    here = parts[0] + parts[2]
    there = parts[1] + parts[3]
    low = jnp.where(core == 0, here, there)
    high = jnp.where(core == 0, there, here)
    for j in range(3):
        span = slice(j * CR, (j + 1) * CR)
        grad_conv[:, j * 128 : (j + 1) * 128] = low[span, :]
        grad_conv[:, (3 + j) * 128 : (4 + j) * 128] = high[span, :]
    for mask in range(4):
        by_head[seq ^ mask] = parts[mask][QOFF:, :]

    def place(index, rows):
        grad_qkv[:, index * 128 : (index + 1) * 128] = rows

    for h in range(HEADS):
        place(h, by_head[h, :QR, :])
        place(HEADS + h, by_head[h, QR : 2 * QR, :])
    value_units(
        lambda index, rows: place(2 * HEADS + index, rows),
        [[by_head[h, (2 + k) * QR : (3 + k) * QR, :] for k in range(2)] for h in range(HEADS)],
    )


def last_stage(where, parts):
    return pl.pallas_call(
        last_kernel,
        in_specs=[SMEM] + [VMEM] * 4,
        out_specs=[VMEM] * 2,
        out_shape=[shape((CR, C), F32), shape((QR, 1792), F32)],
        scratch_shapes=[pltpu.VMEM((HEADS, 4 * QR, 128), F32)],
        compiler_params=params(4),
        name="last_stage",
    )(where, *parts)


def attended_kernel(where, a0, a1, a2, a3, out, by_head):
    for mask, ref in enumerate((a0, a1, a2, a3)):
        by_head[where[0] ^ mask] = ref[...]

    def place(index, rows):
        out[:, index * 128 : (index + 1) * 128] = rows

    value_units(
        place, [[by_head[h, :, k * HK : (k + 1) * HK] for k in range(2)] for h in range(HEADS)]
    )


def attended_rows(where, parts):
    return pl.pallas_call(
        attended_kernel,
        in_specs=[SMEM] + [VMEM] * 4,
        out_specs=VMEM,
        out_shape=shape((PAIRS, C)),
        scratch_shapes=[pltpu.VMEM((HEADS, PAIRS, WIN), BF16)],
        compiler_params=params(4),
        name="attended_rows",
    )(where, *parts)


def shards(embedded, conv_weight, qkv_weight, cotangent):
    own = embedded[0]
    seq = lax.axis_index("seq")
    batch = lax.axis_index("batch")
    core, chip = seq % 2, seq // 2
    where = jnp.stack([seq, core, batch // 16, (batch // 4) % 4, batch % 4]).astype(jnp.int32)

    edge = jnp.where(chip == 0, own[-8:], own[:8])
    own, edge = lax.optimization_barrier((own, edge))
    edge = lax.ppermute(edge, "seq", [(1, 2), (2, 1)]) + lax.ppermute(
        edge, "seq", [(1, 3), (2, 0)]
    )
    side = swap_seq(own, 1)
    far = swap_seq(own, 2)
    zero = jnp.zeros((8, C), F32)
    own_low = jnp.where(chip == 1, edge.astype(F32), zero)
    own_high = jnp.where(chip == 0, edge.astype(F32), zero)
    inner_last = jnp.where(core == 0, side[-8:], own[-8:]).astype(F32)
    inner_first = jnp.where(core == 0, own[:8], side[:8]).astype(F32)
    far_low = jnp.where(chip == 0, inner_last, zero)
    far_high = jnp.where(chip == 1, inner_first, zero)

    grads = []
    for mask in range(4):
        head = seq ^ mask
        piece = lax.dynamic_slice(cotangent[0], (0, ((3 * head) // 2) * HK), (PAIRS, WIN))
        grads.append(swap_seq(piece, mask) if mask else piece)

    joined_a, proj_a, columns = conv_chip(
        True, where, own, side, own_low, own_high, conv_weight, qkv_weight
    )
    far, proj_a = lax.optimization_barrier((far, proj_a))
    far_side = swap_seq(far, 1)
    joined_b, proj_b = conv_chip(
        False, where, far, far_side, far_low, far_high, conv_weight, qkv_weight
    )

    grad_a, grad_b, att_mine, att_side, att_b = attention(where, proj_a, proj_b, grads)

    far_grad = swap_seq(grad_b, 2)
    side_grad = swap_seq(grad_a, 1)
    qkv_blocks = qkv_gradient(where, joined_a, joined_b, grad_a, grad_b)
    far_grad, _ = lax.optimization_barrier((far_grad, qkv_blocks))
    qkv_blocks = over_plane(qkv_blocks)
    far_side_grad = swap_seq(far_grad, 1)
    conv_blocks = conv_gradient(
        where, (grad_a, side_grad, far_grad, far_side_grad), qkv_weight, columns
    )

    att_b, _ = lax.optimization_barrier((att_b, far_grad))
    att_far = swap_seq(att_b, 2)
    attended = attended_rows(
        where, (att_mine, swap_seq(att_side, 1), att_far[0], swap_seq(att_far[1], 1))
    )

    conv_blocks = sent(conv_blocks[:4], 1) + sent(conv_blocks[4:], 2)
    qkv_sum = sum_stage(where, qkv_blocks)
    conv_blocks, qkv_sum, attended = lax.optimization_barrier((conv_blocks, qkv_sum, attended))
    conv_blocks = second_stage(where, conv_blocks)
    conv_blocks = sent(conv_blocks[:4], 2) + sent(conv_blocks[4:], 1)
    parts = sent(joint_stage(where, qkv_sum, conv_blocks), 0)
    summed = sum(part.astype(F32) for part in parts).astype(BF16)
    grad_conv, grad_qkv = last_stage(
        where, [summed] + [swap_seq(summed, mask) for mask in (1, 2, 3)]
    )
    return attended.reshape(1, PAIRS, HEADS * HV), grad_conv, grad_qkv


def solution(mesh):
    return jax.shard_map(
        shards,
        mesh=mesh,
        in_specs=(P("batch", "seq", None), P(), P(), P("batch", "seq", None)),
        out_specs=(P("batch", "seq", None), P("batch", None), P("batch", None)),
        check_vma=False,
    )
```

```python
import functools
import math

import jax
import jax.numpy as jnp
from jax import lax
from jax.experimental import pallas as pl
from jax.experimental.pallas import tpu as pltpu
from jax.sharding import PartitionSpec as P

HEADS = 4
HK = 128
HV = 192
WIN = 256
HD = 2 * HK + WIN
STEP = 4
C = 768
BINS = 512
PAIRS = 256
CHIP = 512
PAD = 8
CR = 36
QR = 24
QOFF = 112
JR = QOFF + 4 * QR
F32 = jnp.float32
BF16 = jnp.bfloat16

epsilon = 1e-06
temper = 1.0 / math.sqrt(HK)

VMEM = pl.BlockSpec(memory_space=pltpu.VMEM)
SMEM = pl.BlockSpec(memory_space=pltpu.SMEM)
HBM = pl.BlockSpec(memory_space=pltpu.HBM)


def params(mib):
    return pltpu.CompilerParams(vmem_limit_bytes=mib << 20)


def shape(dims, dtype=BF16):
    return jax.ShapeDtypeStruct(dims, dtype)


def cost(flops, nbytes):
    return pl.CostEstimate(flops=flops, bytes_accessed=nbytes, transcendentals=0)


def in_hbm(array):
    return pltpu.with_memory_space_constraint(array, pltpu.HBM)


def dot(a, b, ca=1, cb=0):
    return lax.dot_general(a, b, (((ca,), (cb,)), ((), ())), preferred_element_type=F32)


def swap_seq(block, mask):
    return lax.ppermute(block, "seq", [(i, i ^ mask) for i in range(4)])


def shift_batch(block, axis, distance):
    pairs = []
    for b in range(64):
        place = [b // 16, (b // 4) % 4, b % 4]
        place[axis] = (place[axis] + distance) % 4
        pairs.append((b, place[0] * 16 + place[1] * 4 + place[2]))
    return lax.ppermute(block, "batch", pairs)


def over_plane(blocks):
    groups = [[zh * 16 + place for place in range(16)] for zh in range(4)]
    return lax.all_to_all(
        blocks, "batch", split_axis=0, concat_axis=0, axis_index_groups=groups, tiled=True
    )


def sent(blocks, axis):
    order = (1, 2, 3) if axis else (2, 1, 3)
    return [blocks[0]] + [shift_batch(blocks[d], axis, d) for d in order]


def conv_kernel(keep, where, first, second, low, high, taps_hbm, weight_hbm, joined, proj, *refs):
    columns_hbm = refs[0] if keep else None
    act, stacked, bins, taps, weight, columns, sems, out_sem = refs[-8:]
    seq, core = where[0], where[1]
    loads = [pltpu.make_async_copy(taps_hbm, taps, sems.at[0])]
    for k, column in enumerate(
        (seq, HEADS + seq, 2 * HEADS + (3 * seq) // 2, 2 * HEADS + (3 * seq) // 2 + 1)
    ):
        source = weight_hbm.at[:, pl.ds(pl.multiple_of(column * HK, HK), HK)]
        loads.append(
            pltpu.make_async_copy(source, weight.at[:, k * HK : (k + 1) * HK], sems.at[1 + k])
        )
    for load in loads:
        load.start()
    for j in range(6):
        span = slice(j * 128, (j + 1) * 128)
        bins[j, 0:8, :] = low[:, span]
        here = pl.multiple_of(8 + core * BINS, 8)
        bins[j, pl.ds(here, BINS), :] = first[:, span].astype(F32)
        here = pl.multiple_of(8 + (1 - core) * BINS, 8)
        bins[j, pl.ds(here, BINS), :] = second[:, span].astype(F32)
        bins[j, 8 + 2 * BINS :, :] = high[:, span]

    def stream(parity, start, count):
        place = 8 + 2 * start + parity
        return jnp.concatenate(
            [bins[j, pl.ds(place, count, stride=2), :] for j in range(6)], axis=1
        )

    for parity in range(2):
        for start, count in ((-4, 4), (0, CHIP), (CHIP, 4)):
            act[PAD + start : PAD + start + count, :] = jax.nn.gelu(
                stream(parity, start, count), approximate=True
            )
        if keep and parity:
            pltpu.make_async_copy(columns, columns_hbm.at[0], out_sem).wait()
        for tap in range(3):
            start = PAD + (tap - 1) * (STEP // 2)
            rows = act[start : start + CHIP, :].astype(BF16)
            stacked[parity, :, tap * C : (tap + 1) * C] = rows
            if keep:
                columns[tap * C : (tap + 1) * C, :] = rows.T
        if keep:
            pltpu.make_async_copy(columns, columns_hbm.at[parity], out_sem).start()
        if parity == 0:
            loads[0].wait()
        out = stream(parity, 0, CHIP) + dot(stacked[parity], taps[...])
        joined[:, parity * C : (parity + 1) * C] = out.astype(BF16)
    for load in loads[1:]:
        load.wait()
    proj[...] = dot(joined[...], weight[...])
    if keep:
        pltpu.make_async_copy(columns, columns_hbm.at[1], out_sem).wait()


def conv_chip(keep, where, first, second, low, high, taps, weight):
    return pl.pallas_call(
        functools.partial(conv_kernel, keep),
        in_specs=[SMEM] + [VMEM] * 4 + [HBM] * 2,
        out_specs=[VMEM] * 2 + ([HBM] if keep else []),
        out_shape=[shape((CHIP, 2 * C)), shape((CHIP, HD), F32)]
        + ([pltpu.HBM((2, 3 * C, CHIP), BF16)] if keep else []),
        scratch_shapes=[
            pltpu.VMEM((CHIP + 2 * PAD, C), F32),
            pltpu.VMEM((2, CHIP, 3 * C), BF16),
            pltpu.VMEM((6, 2 * BINS + 16, 128), F32),
            pltpu.VMEM((3 * C, C), BF16),
            pltpu.VMEM((2 * C, HD), BF16),
            pltpu.VMEM((3 * C, CHIP) if keep else (8, 128), BF16),
            pltpu.SemaphoreType.DMA((5,)),
            pltpu.SemaphoreType.DMA,
        ],
        compiler_params=params(22),
        cost_estimate=cost(int(2 * 2 * 1024 * 3 * C * C) + 2 * CHIP * 2 * C * HD, 12 << 20)
        if keep
        else cost(1, 1),
        name="conv_own" if keep else "conv_far",
    )(where, first, second, low, high, in_hbm(taps), in_hbm(weight))


def unit(raw):
    return lax.rsqrt(jnp.mean(raw * raw, axis=-1, keepdims=True) + epsilon)


def unit_back(raw, grad_normed):
    factor = unit(raw)
    grad_f = grad_normed.astype(F32)
    inner = jnp.mean(grad_f * raw, axis=-1, keepdims=True)
    return (factor * grad_f - raw * factor * factor * factor * inner).astype(BF16)


def attention_kernel(
    where, proj_a, proj_b, g0, g1, g2, g3, grad_a, grad_b_hbm, att_mine, side_hbm, att_b_hbm,
    query, key, value, grad, key_sum, value_sum, att_side, att_b, grad_b, sems,
):
    core = where[1]
    lane = lax.broadcasted_iota(jnp.int32, (CHIP, WIN), 1)
    valid = (lane >= 64 * core) & (lane < 64 * core + HV)
    for part, proj in enumerate((proj_a, proj_b)):
        rows = slice(part * CHIP, (part + 1) * CHIP)
        raw = proj[:, :HK]
        query[rows, :] = (raw * unit(raw)).astype(BF16)
        raw = proj[:, HK : 2 * HK]
        key[rows, :] = (raw * unit(raw)).astype(BF16)
        value[rows, :] = jnp.where(valid, proj[:, 2 * HK :], 0.0).astype(BF16)
    for part, pair in enumerate(((g0, g1), (g2, g3))):
        for side in range(2):
            place = pl.multiple_of(part * CHIP + (core ^ side) * PAIRS, PAIRS)
            grad[pl.ds(place, PAIRS), :] = pair[side][...]
    keys, values = key[...], value[...]
    for tile in range(4):
        rows = slice(tile * PAIRS, (tile + 1) * PAIRS)
        local = slice((tile % 2) * PAIRS, (tile % 2 + 1) * PAIRS)
        queries, grads = query[rows, :], grad[rows, :]
        expo = jnp.exp(dot(queries, keys, 1, 1) * temper)
        probs = expo * (1.0 / jnp.sum(expo, axis=-1, keepdims=True))
        probs_b = probs.astype(BF16)
        attended = dot(probs_b, values).astype(BF16)
        if tile < 2:

            @pl.when(core == tile)
            def _():
                att_mine[...] = attended

            @pl.when(core != tile)
            def _():
                att_side[...] = attended
        else:
            att_b[core ^ (tile - 2)] = attended
        grad_value = dot(probs_b, grads, 0, 0)
        grad_probs = dot(grads, values, 1, 1)
        inner = jnp.sum(probs * grad_probs, axis=-1, keepdims=True)
        grad_scores = (probs * (grad_probs - inner) * temper).astype(BF16)
        grad_query = dot(grad_scores, keys).astype(BF16)
        grad_key = dot(grad_scores, queries, 0, 0)
        if tile:
            value_sum[...] += grad_value
            key_sum[...] += grad_key
        else:
            value_sum[...] = grad_value
            key_sum[...] = grad_key
        proj, out = (proj_a, grad_a) if tile < 2 else (proj_b, grad_b)
        out[local, :HK] = unit_back(proj[local, :HK], grad_query)
    stores = [
        pltpu.make_async_copy(att_side, side_hbm, sems.at[0]),
        pltpu.make_async_copy(att_b, att_b_hbm, sems.at[1]),
        pltpu.make_async_copy(grad_b, grad_b_hbm, sems.at[2]),
    ]
    stores[0].start()
    stores[1].start()
    for part, proj, out in ((1, proj_b, grad_b), (0, proj_a, grad_a)):
        rows = slice(part * CHIP, (part + 1) * CHIP)
        out[:, HK : 2 * HK] = unit_back(proj[:, HK : 2 * HK], key_sum[rows, :].astype(BF16))
        out[:, 2 * HK :] = jnp.where(valid, value_sum[rows, :], 0.0).astype(BF16)
        if part:
            stores[2].start()
    for store in stores:
        store.wait()


def attention(where, proj_a, proj_b, grads):
    return pl.pallas_call(
        attention_kernel,
        in_specs=[SMEM] + [VMEM] * 6,
        out_specs=[VMEM, HBM, VMEM, HBM, HBM],
        out_shape=[
            shape((CHIP, HD)),
            pltpu.HBM((CHIP, HD), BF16),
            shape((PAIRS, WIN)),
            pltpu.HBM((PAIRS, WIN), BF16),
            pltpu.HBM((2, PAIRS, WIN), BF16),
        ],
        scratch_shapes=[
            pltpu.VMEM((2 * CHIP, HK), BF16),
            pltpu.VMEM((2 * CHIP, HK), BF16),
            pltpu.VMEM((2 * CHIP, WIN), BF16),
            pltpu.VMEM((2 * CHIP, WIN), BF16),
            pltpu.VMEM((2 * CHIP, HK), F32),
            pltpu.VMEM((2 * CHIP, WIN), F32),
            pltpu.VMEM((PAIRS, WIN), BF16),
            pltpu.VMEM((2, PAIRS, WIN), BF16),
            pltpu.VMEM((CHIP, HD), BF16),
            pltpu.SemaphoreType.DMA((3,)),
        ],
        compiler_params=params(20),
        cost_estimate=cost(6 * 2 * 1024 * 1024 * 192, 6 << 20),
        name="attention",
    )(where, proj_a, proj_b, *grads)


def qkv_kernel(where, joined_a, joined_b, grad_a, grad_b, out_hbm, staged, sems):
    low = where[1] == 0
    for first in range(2):
        loose = []
        for zh in (first, first + 2):
            columns = slice(zh * 16 * QR, (zh + 1) * 16 * QR)
            table = dot(joined_a[:, columns], grad_a[...], 0, 0) + dot(
                joined_b[:, columns], grad_b[...], 0, 0
            )
            lower, upper = table[:, 256:384], table[:, 384:]
            panels = (table[:, :128], table[:, 128:256], jnp.where(low, lower, upper))
            loose.append(jnp.where(low, upper, lower))
            for k, panel in enumerate(panels):
                rows = panel.astype(BF16)
                span = slice((4 * k + zh) * QR, (4 * k + zh + 1) * QR)
                for place in range(16):
                    staged[place, span, :] = rows[place * QR : (place + 1) * QR, :]
        turned = [pltpu.roll(half, 64, 1) for half in loose]
        rows = (jnp.where(low, loose[0], turned[0]) + jnp.where(low, turned[1], loose[1])).astype(
            BF16
        )
        span = slice((12 + first) * QR, (13 + first) * QR)
        for place in range(16):
            staged[place, span, :] = rows[place * QR : (place + 1) * QR, :]
    store = pltpu.make_async_copy(staged, out_hbm, sems)
    store.start()
    store.wait()


def qkv_gradient(where, joined_a, joined_b, grad_a, grad_b):
    return pl.pallas_call(
        qkv_kernel,
        in_specs=[SMEM] + [VMEM] * 4,
        out_specs=HBM,
        out_shape=pltpu.HBM((16, 14 * QR, 128), BF16),
        scratch_shapes=[
            pltpu.VMEM((16, 14 * QR, 128), BF16),
            pltpu.SemaphoreType.DMA,
        ],
        compiler_params=params(14),
        cost_estimate=cost(2 * 1536 * 1024 * HD, 6 << 20),
        name="qkv_gradient",
    )(where, joined_a, joined_b, grad_a, grad_b)


def value_units(place, heads):
    place(0, heads[0][0])
    place(1, heads[0][1] + heads[1][0])
    place(2, heads[1][1])
    place(3, heads[2][0])
    place(4, heads[2][1] + heads[3][0])
    place(5, heads[3][1])


def conv_gradient_kernel(where, g0, g1, g2, g3, weight_hbm, columns_hbm, *refs):
    out_x, out_y = refs[:4], refs[4:8]
    by_head, natural, weight, columns, table, pieces, sems = refs[8:]
    seq, core, x, y = where[0], where[1], where[3], where[4]
    half = C // 2
    loads = []
    for p in range(2):
        source = weight_hbm.at[pl.ds(pl.multiple_of(p * C + core * half, half), half), :]
        loads.append(
            pltpu.make_async_copy(source, weight.at[p * half : (p + 1) * half, :], sems.at[p])
        )
    for p in range(2):
        loads.append(pltpu.make_async_copy(columns_hbm.at[p], columns.at[p], sems.at[2 + p]))
    for load in loads:
        load.start()
    for mask, ref in enumerate((g0, g1, g2, g3)):
        by_head[seq ^ mask] = ref[...]
    for h in range(HEADS):
        natural[:, h * HK : (h + 1) * HK] = by_head[h, :, :HK]
        natural[:, (HEADS + h) * HK : (HEADS + h + 1) * HK] = by_head[h, :, HK : 2 * HK]

    def place(index, rows):
        natural[:, (2 * HEADS + index) * HK : (2 * HEADS + index + 1) * HK] = rows

    value_units(
        place, [[by_head[h, :, (2 + k) * HK : (3 + k) * HK] for k in range(2)] for h in range(HEADS)]
    )
    loads[0].wait()
    loads[1].wait()
    hidden = dot(natural[...], weight[...], 1, 1).astype(BF16)
    loads[2].wait()
    loads[3].wait()
    block = 4 * CR
    for zh in range(4):
        rows = slice(zh * 4 * block, (zh + 1) * 4 * block)
        table[...] = dot(columns[0, rows, :], hidden[:, :half]) + dot(
            columns[1, rows, :], hidden[:, half:]
        )
        if zh < 2:
            for d in range(4):
                begin = pl.multiple_of(((x + d) % 4) * block, 8)
                out_x[d][zh] = table[pl.ds(begin, block), :].astype(BF16)
        else:
            for xx in range(4):
                chunk = table[xx * block : (xx + 1) * block, :]
                for yy in range(4):
                    pieces[(yy - y + 4) % 4, zh - 2, xx * CR : (xx + 1) * CR, :] = chunk[
                        yy * CR : (yy + 1) * CR, :
                    ]
    for d in range(4):
        out_y[d][...] = pieces[d].astype(BF16)


def conv_gradient(where, grads, weight, columns):
    return pl.pallas_call(
        conv_gradient_kernel,
        in_specs=[SMEM] + [VMEM] * 4 + [HBM] * 2,
        out_specs=[VMEM] * 8,
        out_shape=[shape((2, 4 * CR, C // 2))] * 8,
        scratch_shapes=[
            pltpu.VMEM((HEADS, CHIP, HD), BF16),
            pltpu.VMEM((CHIP, 1792), BF16),
            pltpu.VMEM((C, 1792), BF16),
            pltpu.VMEM((2, 3 * C, CHIP), BF16),
            pltpu.VMEM((16 * CR, C // 2), F32),
            pltpu.VMEM((4, 2, 4 * CR, C // 2), F32),
            pltpu.SemaphoreType.DMA((4,)),
        ],
        compiler_params=params(20),
        cost_estimate=cost(int(0.3 * (2 * CHIP * 1792 * C + 2 * 1024 * 3 * C * C // 2)), 1 << 20),
        name="conv_gradient",
    )(where, *grads, in_hbm(weight), in_hbm(columns))


def total(refs):
    out = refs[0][...].astype(F32)
    for ref in refs[1:]:
        out = out + ref[...].astype(F32)
    return out


def second_kernel(where, *refs):
    outs, pieces = refs[8:16], refs[16]
    for half, me in enumerate((where[4], where[3])):
        summed = total(refs[4 * half : 4 * half + 4])
        for k in range(4):
            pieces[(k - me + 4) % 4] = summed[:, k * CR : (k + 1) * CR, :]
        for d in range(4):
            outs[4 * half + d][...] = pieces[d].astype(BF16)


def second_stage(where, blocks):
    dims = (2, CR, C // 2)
    return pl.pallas_call(
        second_kernel,
        in_specs=[SMEM] + [VMEM] * 8,
        out_specs=[VMEM] * 8,
        out_shape=[shape(dims)] * 8,
        scratch_shapes=[pltpu.VMEM((4, *dims), F32)],
        compiler_params=params(10),
        name="second_stage",
    )(where, *blocks)


def sum_kernel(where, blocks, out):
    low = where[1] == 0
    rows = blocks[0].astype(F32)
    for place in range(1, 16):
        rows = rows + blocks[place].astype(F32)
    count = 4 * QR
    full, loose = rows[2 * count : 3 * count, :], rows[3 * count :, :]
    turned = pltpu.roll(loose, 64, 1)
    half = jnp.concatenate([jnp.where(low, loose, turned), jnp.where(low, turned, loose)])
    lane = lax.broadcasted_iota(jnp.int32, half.shape, 1)
    half = jnp.where((lane < 64) == low, half, 0.0)
    out[:, :128] = rows[:count, :]
    out[:, 128:256] = rows[count : 2 * count, :]
    out[:, 256:384] = jnp.where(low, full, half)
    out[:, 384:] = jnp.where(low, half, full)


def sum_stage(where, blocks):
    return pl.pallas_call(
        sum_kernel,
        in_specs=[SMEM, VMEM],
        out_specs=VMEM,
        out_shape=shape((4 * QR, HD), F32),
        compiler_params=params(8),
        name="sum_stage",
    )(where, blocks)


def joint_kernel(where, qkv, *refs):
    conv, outs, pieces = refs[:8], refs[8:12], refs[12]
    halves = [total(conv[:4]), total(conv[4:])]
    for zh in range(4):
        for j in range(3):
            pieces[zh, j * CR : (j + 1) * CR, :] = halves[zh // 2][
                zh % 2, :, j * 128 : (j + 1) * 128
            ]
        pieces[zh, 3 * CR : QOFF, :] = jnp.zeros((QOFF - 3 * CR, 128), F32)
        for j in range(4):
            pieces[zh, QOFF + j * QR : QOFF + (j + 1) * QR, :] = qkv[
                zh * QR : (zh + 1) * QR, j * 128 : (j + 1) * 128
            ]
    for d in range(4):
        outs[d][...] = pieces[(where[2] + d) % 4].astype(BF16)


def joint_stage(where, qkv, conv):
    return pl.pallas_call(
        joint_kernel,
        in_specs=[SMEM] + [VMEM] * 9,
        out_specs=[VMEM] * 4,
        out_shape=[shape((JR, 128))] * 4,
        scratch_shapes=[pltpu.VMEM((4, JR, 128), F32)],
        compiler_params=params(6),
        name="joint_stage",
    )(where, qkv, *conv)


def last_kernel(where, r0, r1, r2, r3, grad_conv, grad_qkv, by_head):
    seq, core = where[0], where[1]
    parts = [ref[...].astype(F32) for ref in (r0, r1, r2, r3)]
    here = parts[0] + parts[2]
    there = parts[1] + parts[3]
    low = jnp.where(core == 0, here, there)
    high = jnp.where(core == 0, there, here)
    for j in range(3):
        span = slice(j * CR, (j + 1) * CR)
        grad_conv[:, j * 128 : (j + 1) * 128] = low[span, :]
        grad_conv[:, (3 + j) * 128 : (4 + j) * 128] = high[span, :]
    for mask in range(4):
        by_head[seq ^ mask] = parts[mask][QOFF:, :]

    def place(index, rows):
        grad_qkv[:, index * 128 : (index + 1) * 128] = rows

    for h in range(HEADS):
        place(h, by_head[h, :QR, :])
        place(HEADS + h, by_head[h, QR : 2 * QR, :])
    value_units(
        lambda index, rows: place(2 * HEADS + index, rows),
        [[by_head[h, (2 + k) * QR : (3 + k) * QR, :] for k in range(2)] for h in range(HEADS)],
    )


def last_stage(where, parts):
    return pl.pallas_call(
        last_kernel,
        in_specs=[SMEM] + [VMEM] * 4,
        out_specs=[VMEM] * 2,
        out_shape=[shape((CR, C), F32), shape((QR, 1792), F32)],
        scratch_shapes=[pltpu.VMEM((HEADS, 4 * QR, 128), F32)],
        compiler_params=params(4),
        name="last_stage",
    )(where, *parts)


def attended_kernel(where, a0, a1, a2, a3, out, by_head):
    for mask, ref in enumerate((a0, a1, a2, a3)):
        by_head[where[0] ^ mask] = ref[...]

    def place(index, rows):
        out[:, index * 128 : (index + 1) * 128] = rows

    value_units(
        place, [[by_head[h, :, k * HK : (k + 1) * HK] for k in range(2)] for h in range(HEADS)]
    )


def attended_rows(where, parts):
    return pl.pallas_call(
        attended_kernel,
        in_specs=[SMEM] + [VMEM] * 4,
        out_specs=VMEM,
        out_shape=shape((PAIRS, C)),
        scratch_shapes=[pltpu.VMEM((HEADS, PAIRS, WIN), BF16)],
        compiler_params=params(4),
        name="attended_rows",
    )(where, *parts)


def shards(embedded, conv_weight, qkv_weight, cotangent):
    own = embedded[0]
    seq = lax.axis_index("seq")
    batch = lax.axis_index("batch")
    core, chip = seq % 2, seq // 2
    where = jnp.stack([seq, core, batch // 16, (batch // 4) % 4, batch % 4]).astype(jnp.int32)

    edges = jnp.concatenate([own[:8], own[-8:]])
    own, edges = lax.optimization_barrier((own, edges))
    edge_same, edge_other = swap_seq(edges, 2), swap_seq(edges, 3)
    side = swap_seq(own, 1)
    far = swap_seq(own, 2)
    zero = jnp.zeros((8, C), F32)
    first = lambda a, b: jnp.where(core == 0, a, b)[:8].astype(F32)
    last = lambda a, b: jnp.where(core == 0, b, a)[8:].astype(F32)
    side_edges = jnp.concatenate([side[:8], side[-8:]])
    own_low = jnp.where(chip == 1, last(edge_same, edge_other), zero)
    own_high = jnp.where(chip == 0, first(edge_same, edge_other), zero)
    far_low = jnp.where(chip == 0, last(edges, side_edges), zero)
    far_high = jnp.where(chip == 1, first(edges, side_edges), zero)

    grads = []
    for mask in range(4):
        head = seq ^ mask
        piece = lax.dynamic_slice(cotangent[0], (0, ((3 * head) // 2) * HK), (PAIRS, WIN))
        grads.append(swap_seq(piece, mask) if mask else piece)

    joined_a, proj_a, columns = conv_chip(
        True, where, own, side, own_low, own_high, conv_weight, qkv_weight
    )
    far, proj_a = lax.optimization_barrier((far, proj_a))
    far_side = swap_seq(far, 1)
    joined_b, proj_b = conv_chip(
        False, where, far, far_side, far_low, far_high, conv_weight, qkv_weight
    )

    grad_a, grad_b, att_mine, att_side, att_b = attention(where, proj_a, proj_b, grads)

    far_grad = swap_seq(grad_b, 2)
    side_grad = swap_seq(grad_a, 1)
    qkv_blocks = qkv_gradient(where, joined_a, joined_b, grad_a, grad_b)
    far_grad, _ = lax.optimization_barrier((far_grad, qkv_blocks))
    qkv_blocks = over_plane(qkv_blocks)
    far_side_grad = swap_seq(far_grad, 1)
    conv_blocks = conv_gradient(
        where, (grad_a, side_grad, far_grad, far_side_grad), qkv_weight, columns
    )

    att_b, _ = lax.optimization_barrier((att_b, far_grad))
    att_far = swap_seq(att_b, 2)
    attended = attended_rows(
        where, (att_mine, swap_seq(att_side, 1), att_far[0], swap_seq(att_far[1], 1))
    )

    conv_blocks = sent(conv_blocks[:4], 1) + sent(conv_blocks[4:], 2)
    qkv_sum = sum_stage(where, qkv_blocks)
    conv_blocks, qkv_sum, attended = lax.optimization_barrier((conv_blocks, qkv_sum, attended))
    conv_blocks = second_stage(where, conv_blocks)
    conv_blocks = sent(conv_blocks[:4], 2) + sent(conv_blocks[4:], 1)
    parts = sent(joint_stage(where, qkv_sum, conv_blocks), 0)
    summed = sum(part.astype(F32) for part in parts).astype(BF16)
    grad_conv, grad_qkv = last_stage(
        where, [summed] + [swap_seq(summed, mask) for mask in (1, 2, 3)]
    )
    return attended.reshape(1, PAIRS, HEADS * HV), grad_conv, grad_qkv


def solution(mesh):
    return jax.shard_map(
        shards,
        mesh=mesh,
        in_specs=(P("batch", "seq", None), P(), P(), P("batch", "seq", None)),
        out_specs=(P("batch", "seq", None), P("batch", None), P("batch", None)),
        check_vma=False,
    )
```
